768 devices in a mesh: ctx: 64 (over x, y, core), head: 12 (over z).
Axes of the slice: x: 4, y: 8, z: 12, core: 2. Of those that a mesh axis runs over, the one named last changes fastest.
Arguments:
- prompt_q: bfloat16 [8192, 36, 128], P('ctx', 'head'), may hold values from -6 to 6
- prompt_k: bfloat16 [8192, 36, 128], P('ctx', 'head'), may hold values from -6 to 6
- prompt_v: bfloat16 [8192, 36, 128], P('ctx', 'head'), may hold values from -6 to 6
- resp_q: bfloat16 [2, 4096, 36, 128], P(None, 'ctx', 'head'), may hold values from -6 to 6
- resp_k: bfloat16 [2, 4096, 36, 128], P(None, 'ctx', 'head'), may hold values from -6 to 6
- resp_v: bfloat16 [2, 4096, 36, 128], P(None, 'ctx', 'head'), may hold values from -6 to 6
- decay_rate: float32 [36], P('head'), may hold values from 8.138021e-06 to 0.033
- norm_gain: float32 [36, 128], P('head'), may hold values from 0.1 to 1.9
- prompt_cot: bfloat16 [8192, 36, 128], P('ctx', 'head'), may hold values from -6 to 6
- resp_cot: bfloat16 [2, 4096, 36, 128], P(None, 'ctx', 'head'), may hold values from -6 to 6
Outputs:
- prompt_y: bfloat16 [8192, 36, 128], P('ctx', 'head')
- resp_y: bfloat16 [2, 4096, 36, 128], P(None, 'ctx', 'head')
- prompt_dq: bfloat16 [8192, 36, 128], P('ctx', 'head')
- prompt_dk: bfloat16 [8192, 36, 128], P('ctx', 'head')
- prompt_dv: bfloat16 [8192, 36, 128], P('ctx', 'head')
- resp_dq: bfloat16 [2, 4096, 36, 128], P(None, 'ctx', 'head')
- resp_dk: bfloat16 [2, 4096, 36, 128], P(None, 'ctx', 'head')
- resp_dv: bfloat16 [2, 4096, 36, 128], P(None, 'ctx', 'head')
The draws below stay inside these ranges and needn't reach their ends.
All inputs are finite; a program needn't handle non-finite values.
Results may differ from the reference program's by a relative error of at most 0.0062.
Values sent between devices are 32-bit elements; how exact they have to be, the bound alone decides.
A program may use at most 128 MiB of HBM per device.

```python
import math
import jax
import jax.numpy as jnp
from jax import lax

DK = 128
BLK = 64
RESPONSES = 2
HEADS = 36
TOKENS = 8192
RESP = 4096


def block_levels(rng, dims, shards, smallest, top_value):
    factor_of = 1.0
    for dim, shards_of in shards:
        steps = jax.random.uniform(jax.random.fold_in(jax.random.fold_in(rng, 6), dim), (shards_of,), jnp.float32, smallest / len(shards), top_value / len(shards))
        factor_of = factor_of * jnp.repeat(jnp.exp(steps), dims[dim] // shards_of).reshape((-1,) + (1,) * (len(dims) - 1 - dim))
    return factor_of


def noise(rng, extent, width, bound, split=(), kind=jnp.bfloat16):
    values = jax.random.normal(rng, extent, jnp.float32) * width
    if len(split) > 0:
        values = block_levels(rng, extent, split, -0.22, 0.18) * values
    return jnp.clip(values, min=-bound, max=bound).astype(kind)


def setup_inputs(seed: int = 0) -> dict:
    seeds = jax.random.split(jax.random.key(seed), 11)
    prompt_q = noise(seeds[0], (TOKENS, HEADS, DK), 1.0, 6.0, ((0, 64), (1, 12)))
    prompt_k = noise(seeds[1], (TOKENS, HEADS, DK), 1.0, 6.0, ((0, 64), (1, 12)))
    prompt_v = noise(seeds[2], (TOKENS, HEADS, DK), 1.0, 6.0, ((0, 64), (1, 12)))
    resp_q = noise(seeds[3], (RESPONSES, RESP, HEADS, DK), 1.0, 6.0, ((1, 64), (2, 12)))
    resp_k = noise(seeds[4], (RESPONSES, RESP, HEADS, DK), 1.0, 6.0, ((1, 64), (2, 12)))
    resp_v = noise(seeds[5], (RESPONSES, RESP, HEADS, DK), 1.0, 6.0, ((1, 64), (2, 12)))
    decay_rate = jnp.clip(jnp.exp(math.log(0.033) - 8.3077158 * jax.random.uniform(seeds[6], (HEADS,), jnp.float32) ** block_levels(seeds[6], (HEADS,), ((0, 12),), -0.2, 0.2)), 8.138021257764194e-06, 0.033)
    norm_gain = jnp.clip(1.0 + 0.18 * jax.random.normal(seeds[7], (HEADS, DK), jnp.float32), 0.1, 1.9)
    prompt_cot = noise(seeds[8], (TOKENS, HEADS, DK), 1.0, 6.0, ((0, 64), (1, 12)))
    resp_cot = noise(seeds[9], (RESPONSES, RESP, HEADS, DK), 1.0, 6.0, ((1, 64), (2, 12)))
    return {"prompt_q": prompt_q, "prompt_k": prompt_k, "prompt_v": prompt_v, "resp_q": resp_q, "resp_k": resp_k, "resp_v": resp_v, "decay_rate": decay_rate, "norm_gain": norm_gain, "prompt_cot": prompt_cot, "resp_cot": resp_cot}


F32 = jnp.float32
BF16 = jnp.bfloat16

def contract(form, left, right):
    return jnp.einsum(form, left.astype(F32), right.astype(F32), precision=lax.Precision.HIGHEST)

def powers(rates, steps):
    return jnp.exp(-rates[:, None] * steps[None, :])

def decay_mask(rates, length):
    places = jnp.arange(length, dtype=F32)
    offset = places[:, None] - places[None, :]
    decays = jnp.exp(-rates[:, None, None] * jnp.maximum(offset, 0.0)[None])
    return jnp.where((offset >= 0.0)[None], decays, 0.0)

def key_term(keys, values, rates):
    length = keys.shape[0]
    places = jnp.arange(length, dtype=F32)
    factor = powers(rates, length - 1.0 - places).T[:, :, None]
    keys_decayed = (keys.astype(F32) * factor).astype(BF16)
    return contract('shd,she->hde', keys_decayed, values)

def query_term(queries, grad_out, rates):
    length = queries.shape[0]
    places = jnp.arange(length, dtype=F32)
    factor = powers(rates, places + 1.0).T[:, :, None]
    queries_decayed = (queries.astype(F32) * factor).astype(BF16)
    return contract('jhd,jhe->hde', queries_decayed, grad_out)

def block_forward(queries, keys, values, carried, rates):
    length = queries.shape[0]
    places = jnp.arange(length, dtype=F32)
    scores = contract('jhd,shd->hjs', queries, keys)
    mixing = (scores * decay_mask(rates, length)).astype(BF16)
    within = contract('hjs,shd->jhd', mixing, values)
    across = contract('jhd,hde->jhe', queries, carried.astype(BF16)) * powers(rates, places + 1.0).T[:, :, None]
    following = jnp.exp(-rates * length)[:, None, None] * carried + key_term(keys, values, rates)
    return (within + across, following)

def block_backward(queries, keys, values, grad_out, carried, later_grad, rates):
    length = queries.shape[0]
    places = jnp.arange(length, dtype=F32)
    masking = decay_mask(rates, length)
    mixing = (contract('jhd,shd->hjs', queries, keys) * masking).astype(BF16)
    dmixing = (contract('jhe,she->hjs', grad_out, values) * masking).astype(BF16)
    query_decay = powers(rates, places + 1.0).T[:, :, None]
    key_decay = powers(rates, length - 1.0 - places).T[:, :, None]
    later_bf = later_grad.astype(BF16)
    grad_q = contract('hjs,shd->jhd', dmixing, keys) + query_decay * contract('jhe,hde->jhd', grad_out, carried.astype(BF16))
    grad_k = contract('hjs,jhd->shd', dmixing, queries) + key_decay * contract('she,hde->shd', values, later_bf)
    grad_v = contract('hjs,jhe->she', mixing, grad_out) + key_decay * contract('shd,hde->she', keys, later_bf)
    earlier = jnp.exp(-rates * length)[:, None, None] * later_grad + query_term(queries, grad_out, rates)
    return (grad_q, grad_k, grad_v, earlier)

def split_blocks(array, block):
    return array.reshape((array.shape[0] // block, block) + array.shape[1:])

def chain_forward(queries, keys, values, carried, rates, block):

    def advance(state_now, pieces):
        outputs, following = block_forward(pieces[0], pieces[1], pieces[2], state_now, rates)
        return (following, (outputs, state_now))
    pieces = (split_blocks(queries, block), split_blocks(keys, block), split_blocks(values, block))
    final_state, (outputs, entries) = lax.scan(advance, carried, pieces)
    return (outputs.reshape(queries.shape), entries, final_state)

def chain_backward(queries, keys, values, grad_out, entries, later_grad, rates, block):

    def retreat(grad_now, pieces):
        grad_q, grad_k, grad_v, earlier = block_backward(pieces[0], pieces[1], pieces[2], pieces[3], pieces[4], grad_now, rates)
        return (earlier, (grad_q, grad_k, grad_v))
    pieces = (split_blocks(queries, block), split_blocks(keys, block), split_blocks(values, block), split_blocks(grad_out, block), entries)
    start_grad, (grad_q, grad_k, grad_v) = lax.scan(retreat, later_grad, pieces, reverse=True)
    return (grad_q.reshape(queries.shape), grad_k.reshape(queries.shape), grad_v.reshape(queries.shape), start_grad)

def norm_sums(outputs, cotangent, norm_gain):
    square_sum = lax.optimization_barrier(jnp.sum(outputs * outputs, axis=(1, 2)))
    inner_sum = lax.optimization_barrier(jnp.sum(norm_gain[None] * cotangent.astype(F32) * outputs, axis=(1, 2)))
    return (square_sum, inner_sum)

def norm_finish(outputs, cotangent, norm_gain, square_sum, inner_sum, features):
    inv_rms = lax.rsqrt(square_sum / features + 1e-05)[:, None, None]
    normed = (norm_gain[None] * outputs * inv_rms).astype(BF16)
    cubed = inv_rms * inv_rms * inv_rms
    grad = (norm_gain[None] * cotangent.astype(F32) * inv_rms - outputs * inner_sum[:, None, None] * cubed / features).astype(BF16)
    return (normed, grad)

def reference(prompt_q, prompt_k, prompt_v, resp_q, resp_k, resp_v, decay_rate, norm_gain, prompt_cot, resp_cot):
    zero_state = jnp.zeros((HEADS, DK, DK), F32)
    features = HEADS * DK
    prompt_out, prompt_entries, final_state = chain_forward(prompt_q, prompt_k, prompt_v, zero_state, decay_rate, BLK)

    def respond(pieces):
        outputs, entries, ignored = chain_forward(pieces[0], pieces[1], pieces[2], final_state, decay_rate, BLK)
        return (outputs, entries)
    resp_out, resp_entries = lax.map(respond, (resp_q, resp_k, resp_v))
    square_sum, inner_sum = norm_sums(prompt_out, prompt_cot, norm_gain)
    prompt_y, prompt_grad = norm_finish(prompt_out, prompt_cot, norm_gain, square_sum, inner_sum, features)
    flat_out = resp_out.reshape((RESPONSES * RESP, HEADS, DK))
    flat_cot = resp_cot.reshape((RESPONSES * RESP, HEADS, DK))
    square_sum, inner_sum = norm_sums(flat_out, flat_cot, norm_gain)
    resp_y, resp_grad = norm_finish(flat_out, flat_cot, norm_gain, square_sum, inner_sum, features)
    resp_y = resp_y.reshape(resp_q.shape)
    resp_grad = resp_grad.reshape(resp_q.shape)

    def retract(pieces):
        return chain_backward(pieces[0], pieces[1], pieces[2], pieces[3], pieces[4], zero_state, decay_rate, BLK)
    resp_dq, resp_dk, resp_dv, starts = lax.map(retract, (resp_q, resp_k, resp_v, resp_grad, resp_entries))
    total_grad = lax.optimization_barrier(jnp.sum(starts, axis=0))
    prompt_dq, prompt_dk, prompt_dv, ignored = chain_backward(prompt_q, prompt_k, prompt_v, prompt_grad, prompt_entries, total_grad, decay_rate, BLK)
    return (prompt_y, resp_y, prompt_dq.astype(BF16), prompt_dk.astype(BF16), prompt_dv.astype(BF16), resp_dq.astype(BF16), resp_dk.astype(BF16), resp_dv.astype(BF16))
```

```python
import functools

import jax
import jax.numpy as jnp
from jax import lax
from jax.experimental import pallas as pl
from jax.experimental.pallas import tpu as pltpu
from jax.sharding import PartitionSpec as P

GRID = (4, 8, 2)
MESH = pl.DeviceIdType.MESH
F32 = jnp.float32
BF16 = jnp.bfloat16


def dot(left, right, dims):
    return lax.dot_general(left, right, (dims, ((), ())), preferred_element_type=F32)


def dot_nn(left, right):
    return dot(left, right, ((1,), (0,)))


def dot_nt(left, right):
    return dot(left, right, ((1,), (1,)))


def dot_tn(left, right):
    return dot(left, right, ((0,), (0,)))


class Place:
    def __init__(self, grid, reverse):
        self.nx, self.ny, _ = grid
        self.reverse = reverse
        ctx = lax.axis_index("ctx")
        self.head = lax.axis_index("head")
        self.core = lax.rem(ctx, 2)
        self.phys_y = lax.rem(ctx // 2, self.ny)
        self.phys_x = ctx // (2 * self.ny)
        self.y = self.ny - 1 - self.phys_y if reverse else self.phys_y
        self.x = self.nx - 1 - self.phys_x if reverse else self.phys_x
        self.order = 1 - self.core if reverse else self.core

    def device(self, x, y, core):
        return ((x * self.ny + y) * 2 + core, self.head)

    def partner(self):
        return self.device(self.phys_x, self.phys_y, 1 - self.core)

    def along_y(self, y):
        return self.device(self.phys_x, self.ny - 1 - y if self.reverse else y, self.core)

    def along_x(self, x):
        return self.device(self.nx - 1 - x if self.reverse else x, self.phys_y, self.core)


class Scan:
    def __init__(self, way, place, rate, lengths, refs, pending):
        self.way, self.place, self.rate, self.lengths = way, place, rate, lengths
        (self.loc, self.pair, self.csend, self.a1, self.tx, self.psend, self.a2, self.fsend, self.st) = refs[:9]
        (self.c_s, self.c_r, self.a1_s, self.a1_r, self.x_s, self.x_r, self.a2_s, self.a2_r, self.f_s, self.f_r) = refs[9:]
        self.pending = pending
        self.rows = self.csend.shape[4]
        self.half = self.fsend.shape[3]

    def decay(self, h, tokens):
        return jnp.exp(jnp.full((1, 128), -self.rate[h], F32) * tokens)

    def copy(self, src, dst, send, recv, device):
        return pltpu.make_async_remote_copy(
            src_ref=src, dst_ref=dst, send_sem=send, recv_sem=recv, device_id=device, device_id_type=MESH
        )

    def start(self, copy):
        copy.start()
        self.pending.append(copy)

    def own_half(self):
        return pl.ds(pl.multiple_of(self.place.core * self.half, self.half), self.half)

    def pair_copy(self, h):
        w, p = self.way, self.place
        other = pl.ds(pl.multiple_of((1 - p.core) * self.half, self.half), self.half)
        return self.copy(
            self.loc.at[w, h, :, other, :], self.pair.at[w, h], self.c_s.at[w, h], self.c_r.at[w, h], p.partner()
        )

    def start_pair(self, h):
        self.start(self.pair_copy(h))

    def first_second(self, h, s):
        own = self.loc[self.way, h, s, self.own_half(), :]
        other = self.pair[self.way, h, s]
        leads = self.place.order == 0
        return jnp.where(leads, own, other), jnp.where(leads, other, own)

    def gather_copy(self, h, k):
        w, p = self.way, self.place
        to = lax.rem(p.y + k, p.ny)
        return self.copy(
            self.csend.at[w, h, to], self.a1.at[w, h, p.y], self.a1_s.at[w, h, k], self.a1_r.at[w, h, p.y], p.along_y(to)
        )

    def chip(self, h):
        w, p = self.way, self.place
        self.pair_copy(h).wait_recv()
        for s, length in enumerate(self.lengths):
            first, second = self.first_second(h, s)
            both = self.decay(h, float(length)) * first + second
            for j in range(p.ny):
                self.csend[w, h, j, s] = both[j * self.rows : (j + 1) * self.rows]
        self.a1[w, h, p.y] = self.csend[w, h, p.y]
        for k in far_first(p.ny):
            self.start(self.gather_copy(h, k))

    def wait_along(self, buf, sem, here, n, h, device):
        w = self.way
        for k in range(1, n):
            source = lax.rem(here + k, n)
            self.copy(
                buf.at[w, h, source], buf.at[w, h, source], sem.at[w, h, source], sem.at[w, h, source], device(source)
            ).wait_recv()

    def column(self, h):
        w, p = self.way, self.place
        self.wait_along(self.a1, self.a1_r, p.y, p.ny, h, p.along_y)
        for s, length in enumerate(self.lengths):
            step = self.decay(h, 2.0 * length)
            total = self.a1[w, h, 0, s]
            for j in range(1, p.ny):
                total = step * total + self.a1[w, h, j, s]
            self.tx[w, h, p.x, s] = total
        for k in far_first(p.nx):
            to = lax.rem(p.x + k, p.nx)
            self.start(
                self.copy(
                    self.tx.at[w, h, p.x], self.tx.at[w, h, p.x], self.x_s.at[w, h, k], self.x_r.at[w, h, p.x], p.along_x(to)
                )
            )

    def spread(self, h, sources, targets):
        w, p = self.way, self.place
        self.wait_along(self.tx, self.x_r, p.x, p.nx, h, p.along_x)
        bases, totals = [], []
        for s, length in enumerate(self.lengths):
            step = self.decay(h, 2.0 * length * p.ny)
            run = self.tx[w, h, 0, s]
            base = jnp.zeros_like(run)
            for j in range(1, p.nx):
                base = jnp.where(p.x == j, run, base)
                run = step * run + self.tx[w, h, j, s]
            bases.append(base)
            totals.append(run)
        given = sum(totals[s] for s in sources)
        for s in targets:
            before = (p.x * (2 * p.ny * self.lengths[s])).astype(F32)
            bases[s] = bases[s] + self.decay(h, before) * given
        for s, length in enumerate(self.lengths):
            step = self.decay(h, 2.0 * length)
            entry = bases[s]
            for j in range(p.ny):
                self.psend[w, h, j, s] = entry
                if j < p.ny - 1:
                    entry = step * entry + self.a1[w, h, j, s]
        self.a2[w, h, p.y] = self.psend[w, h, p.y]
        for k in far_first(p.ny):
            to = lax.rem(p.y + k, p.ny)
            self.start(
                self.copy(
                    self.psend.at[w, h, to], self.a2.at[w, h, p.y], self.a2_s.at[w, h, k], self.a2_r.at[w, h, p.y], p.along_y(to)
                )
            )

    def final_copy(self, h):
        w, p = self.way, self.place
        return self.copy(
            self.fsend.at[w, h], self.st.at[w, h, :, self.own_half(), :], self.f_s.at[w, h], self.f_r.at[w, h], p.partner()
        )

    def finish(self, h):
        w, p = self.way, self.place
        self.wait_along(self.a2, self.a2_r, p.y, p.ny, h, p.along_y)
        leads = p.order == 0
        for s, length in enumerate(self.lengths):
            entry = jnp.concatenate([self.a2[w, h, j, s] for j in range(p.ny)], axis=0)
            first, _ = self.first_second(h, s)
            after = self.decay(h, float(length)) * entry + first
            self.st[w, h, s, self.own_half(), :] = jnp.where(leads, entry, after)
            self.fsend[w, h, s] = jnp.where(leads, after, entry)
        self.start(self.final_copy(h))

    def ready(self, h):
        w, p = self.way, self.place
        other = pl.ds(pl.multiple_of((1 - p.core) * self.half, self.half), self.half)
        landed = self.st.at[w, h, :, other, :]
        self.copy(landed, landed, self.f_r.at[w, h], self.f_r.at[w, h], p.partner()).wait_recv()

    def exchange(self, heads, sources, targets):
        for h in range(heads + 1):
            if h < heads:
                self.column(h)
            if h > 0:
                self.spread(h - 1, sources, targets)
        for h in range(heads):
            self.finish(h)


def far_first(n):
    return sorted(range(1, n), key=lambda k: -min(k, n - k))


def column_of(row):
    return jnp.broadcast_to(row, (128, 128)).T


def kernel(
    grid, nz, rate, gain, pq, pk, pv, pc, rq, rk, rv, rc,
    py, ry, pdq, pdk, pdv, rdq, rdk, rdv,
    loc, pair, csend, a1, tx, psend, a2, fsend, st, stat, pmix, rmix, pout, rout, pgrad, rgrad, dk_p, dv_p, dk_r, dv_r,
    c_s, c_r, a1_s, a1_r, x_s, x_r, a2_s, a2_r, f_s, f_r, z_s, z_r,
):
    heads, tokens, width = pq.shape
    count = rq.shape[2]
    features = float(heads * nz * width)
    ahead, back = Place(grid, False), Place(grid, True)
    ctx, z = lax.axis_index("ctx"), ahead.head

    barrier = pltpu.get_barrier_semaphore()
    peers = [ahead.partner()]
    peers += [ahead.along_y(lax.rem(ahead.y + k, grid[1])) for k in range(1, grid[1])]
    peers += [ahead.along_x(lax.rem(ahead.x + k, grid[0])) for k in range(1, grid[0])]
    peers += [(ctx, lax.rem(z + k, nz)) for k in range(1, nz)]
    for peer in peers:
        pl.semaphore_signal(barrier, inc=1, device_id=peer, device_id_type=MESH)

    pending = []
    refs = (loc, pair, csend, a1, tx, psend, a2, fsend, st, c_s, c_r, a1_s, a1_r, x_s, x_r, a2_s, a2_r, f_s, f_r)
    lengths = (tokens, count, count)
    fwd = Scan(0, ahead, rate, lengths, refs, pending)
    bwd = Scan(1, back, rate, lengths, refs, pending)

    row = lax.broadcasted_iota(jnp.int32, (128, 128), 0)
    col = lax.broadcasted_iota(jnp.int32, (128, 128), 1)
    lag = (row - col).astype(F32)
    causal = row >= col
    apart = (row // count) != (col // count)
    place_p = row.astype(F32)
    place_r = lax.rem(row, count).astype(F32)

    def power(h, steps):
        return jnp.exp(jnp.full((128, 128), -rate[h], F32) * steps)

    def pairs(ref, h):
        return jnp.concatenate([ref[0, h], ref[1, h]], axis=0)

    def masks(h):
        mask = jnp.where(causal, power(h, jnp.maximum(lag, 0.0)), 0.0)
        return mask, jnp.where(apart, 0.0, mask)

    for h in range(heads):
        keys = (pk[h].astype(F32) * power(h, tokens - 1.0 - place_p)).astype(BF16)
        loc[0, h, 0] = dot_tn(keys, pv[h])
        keys = (pairs(rk, h).astype(F32) * power(h, count - 1.0 - place_r)).astype(BF16)
        for r in range(2):
            loc[0, h, 1 + r] = dot_tn(keys[r * count : (r + 1) * count], rv[r, h])
    pl.semaphore_wait(barrier, len(peers))
    for h in range(heads):
        fwd.start_pair(h)
    for h in range(heads):
        fwd.chip(h)

    for h in range(heads):
        mask_p, mask_r = masks(h)
        pmix[h] = (dot_nt(pq[h], pk[h]) * mask_p).astype(BF16)
        rmix[h] = (dot_nt(pairs(rq, h), pairs(rk, h)) * mask_r).astype(BF16)
        pout[h] = dot_nn(pmix[h], pv[h])
        rout[h] = dot_nn(rmix[h], pairs(rv, h))

    fwd.exchange(heads, (0,), (1, 2))

    sums = [jnp.zeros((128, 128), F32) for _ in range(4)]
    for h in range(heads):
        fwd.ready(h)
        out = pout[h] + power(h, place_p + 1.0) * dot_nn(pq[h], st[0, h, 0].astype(BF16))
        pout[h] = out
        sums[0] += out * out
        sums[1] += gain[h : h + 1] * pc[h].astype(F32) * out
        across = [dot_nn(rq[r, h], st[0, h, 1 + r].astype(BF16)) for r in range(2)]
        out = rout[h] + power(h, place_r + 1.0) * jnp.concatenate(across, axis=0)
        rout[h] = out
        sums[2] += out * out
        sums[3] += gain[h : h + 1] * pairs(rc, h).astype(F32) * out
    lines = [jnp.sum(part.T, axis=0, keepdims=True) for part in sums]
    stat[z] = jnp.concatenate(lines + [jnp.zeros((4, 128), F32)], axis=0)

    for k in far_first(nz):
        to = (ctx, lax.rem(z + k, nz))
        fwd.start(fwd.copy(stat.at[z], stat.at[z], z_s.at[k], z_r.at[z], to))
    for k in range(1, nz):
        source = lax.rem(z + k, nz)
        fwd.copy(stat.at[source], stat.at[source], z_r.at[source], z_r.at[source], (ctx, source)).wait_recv()
    total = stat[0]
    for k in range(1, nz):
        total = total + stat[k]

    def norms(at):
        inv = lax.rsqrt(total[at : at + 1] / features + 1e-05)
        return column_of(inv), column_of(total[at + 1 : at + 2] * inv * inv * inv / features)

    inv_p, coef_p = norms(0)
    inv_r, coef_r = norms(2)
    for h in range(heads):
        grad = (gain[h : h + 1] * pc[h].astype(F32) * inv_p - pout[h] * coef_p).astype(BF16)
        pgrad[h] = grad
        queries = (pq[h].astype(F32) * power(h, place_p + 1.0)).astype(BF16)
        loc[1, h, 0] = dot_tn(queries, grad)
        grad = (gain[h : h + 1] * pairs(rc, h).astype(F32) * inv_r - rout[h] * coef_r).astype(BF16)
        rgrad[h] = grad
        queries = (pairs(rq, h).astype(F32) * power(h, place_r + 1.0)).astype(BF16)
        for r in range(2):
            part = slice(r * count, (r + 1) * count)
            loc[1, h, 1 + r] = dot_tn(queries[part], grad[part])
        bwd.start_pair(h)
    for h in range(heads):
        bwd.chip(h)

    for h in range(heads):
        py[h] = (gain[h : h + 1] * pout[h] * inv_p).astype(BF16)
        normed = (gain[h : h + 1] * rout[h] * inv_r).astype(BF16)
        mask_p, mask_r = masks(h)
        grad = pgrad[h]
        dmix = (dot_nt(grad, pv[h]) * mask_p).astype(BF16)
        across = dot_nt(grad, st[0, h, 0].astype(BF16))
        pdq[h] = (dot_nn(dmix, pk[h]) + power(h, place_p + 1.0) * across).astype(BF16)
        dk_p[h] = dot_tn(dmix, pq[h])
        dv_p[h] = dot_tn(pmix[h], grad)
        grad = rgrad[h]
        dmix = (dot_nt(grad, pairs(rv, h)) * mask_r).astype(BF16)
        across = [dot_nt(grad[r * count : (r + 1) * count], st[0, h, 1 + r].astype(BF16)) for r in range(2)]
        queries = dot_nn(dmix, pairs(rk, h)) + power(h, place_r + 1.0) * jnp.concatenate(across, axis=0)
        dk_r[h] = dot_tn(dmix, pairs(rq, h))
        dv_r[h] = dot_tn(rmix[h], grad)
        for r in range(2):
            part = slice(r * count, (r + 1) * count)
            ry[r, h] = normed[part]
            rdq[r, h] = queries[part].astype(BF16)

    bwd.exchange(heads, (1, 2), (0,))

    for h in range(heads):
        bwd.ready(h)
        later = st[1, h, 0].astype(BF16)
        fade = power(h, tokens - 1.0 - place_p)
        pdk[h] = (dk_p[h] + fade * dot_nt(pv[h], later)).astype(BF16)
        pdv[h] = (dv_p[h] + fade * dot_nn(pk[h], later)).astype(BF16)
        fade = power(h, count - 1.0 - place_r)
        for r in range(2):
            part = slice(r * count, (r + 1) * count)
            later = st[1, h, 1 + r].astype(BF16)
            rdk[r, h] = (dk_r[h, part, :] + fade[part] * dot_nt(rv[r, h], later)).astype(BF16)
            rdv[r, h] = (dv_r[h, part, :] + fade[part] * dot_nn(rk[r, h], later)).astype(BF16)

    for copy in pending:
        copy.wait_send()


def shards(grid, nz, prompt_q, prompt_k, prompt_v, resp_q, resp_k, resp_v, decay_rate, norm_gain, prompt_cot, resp_cot):
    nx, ny, _ = grid
    tokens, heads, width = prompt_q.shape
    count = resp_q.shape[1]
    half, rows = width // 2, width // 2 // ny
    prompt = [jnp.transpose(a, (1, 0, 2)) for a in (prompt_q, prompt_k, prompt_v, prompt_cot)]
    resp = [jnp.transpose(a, (0, 2, 1, 3)) for a in (resp_q, resp_k, resp_v, resp_cot)]
    flat = jax.ShapeDtypeStruct((heads, tokens, width), BF16)
    duo = jax.ShapeDtypeStruct((2, heads, count, width), BF16)
    vmem = pl.BlockSpec(memory_space=pltpu.VMEM)
    block = (heads, tokens, width)
    scratch = [
        pltpu.VMEM((2, heads, 3, width, width), F32),
        pltpu.VMEM((2, heads, 3, half, width), F32),
        pltpu.VMEM((2, heads, ny, 3, rows, width), F32),
        pltpu.VMEM((2, heads, ny, 3, rows, width), F32),
        pltpu.VMEM((2, heads, nx, 3, rows, width), F32),
        pltpu.VMEM((2, heads, ny, 3, rows, width), F32),
        pltpu.VMEM((2, heads, ny, 3, rows, width), F32),
        pltpu.VMEM((2, heads, 3, half, width), F32),
        pltpu.VMEM((2, heads, 3, width, width), F32),
        pltpu.VMEM((nz, 8, width), F32),
        pltpu.VMEM(block, BF16),
        pltpu.VMEM(block, BF16),
        pltpu.VMEM(block, F32),
        pltpu.VMEM(block, F32),
        pltpu.VMEM(block, BF16),
        pltpu.VMEM(block, BF16),
        pltpu.VMEM(block, F32),
        pltpu.VMEM(block, F32),
        pltpu.VMEM(block, F32),
        pltpu.VMEM(block, F32),
    ]
    dma = pltpu.SemaphoreType.DMA
    scratch += [dma((2, heads))] * 2 + [dma((2, heads, ny))] * 2 + [dma((2, heads, nx))] * 2
    scratch += [dma((2, heads, ny))] * 2 + [dma((2, heads))] * 2 + [dma((nz,))] * 2
    out = pl.pallas_call(
        functools.partial(kernel, grid, nz),
        out_shape=(flat, duo, flat, flat, flat, duo, duo, duo),
        in_specs=[pl.BlockSpec(memory_space=pltpu.SMEM)] + [vmem] * 9,
        out_specs=(vmem,) * 8,
        scratch_shapes=scratch,
        compiler_params=pltpu.CompilerParams(collective_id=0, has_side_effects=True),
    )(decay_rate, norm_gain, *prompt, *resp)
    return tuple(
        jnp.transpose(a, (1, 0, 2)) if a.ndim == 3 else jnp.transpose(a, (0, 2, 1, 3)) for a in out
    )


def solution(mesh):
    flat, duo = P("ctx", "head", None), P(None, "ctx", "head", None)
    return jax.shard_map(
        functools.partial(shards, GRID, mesh.shape["head"]),
        mesh=mesh,
        in_specs=(flat, flat, flat, duo, duo, duo, P("head"), P("head", None), flat, duo),
        out_specs=(flat, duo, flat, flat, flat, duo, duo, duo),
        check_vma=False,
    )
```

```python
import functools

import jax
import jax.numpy as jnp
from jax import lax
from jax.experimental import pallas as pl
from jax.experimental.pallas import tpu as pltpu
from jax.sharding import PartitionSpec as P

GRID = (4, 8, 2)
MESH = pl.DeviceIdType.MESH
F32 = jnp.float32
BF16 = jnp.bfloat16


def dot(left, right, dims):
    return lax.dot_general(left, right, (dims, ((), ())), preferred_element_type=F32)


def dot_nn(left, right):
    return dot(left, right, ((1,), (0,)))


def dot_nt(left, right):
    return dot(left, right, ((1,), (1,)))


def dot_tn(left, right):
    return dot(left, right, ((0,), (0,)))


class Place:
    def __init__(self, grid, reverse):
        self.nx, self.ny, _ = grid
        self.reverse = reverse
        ctx = lax.axis_index("ctx")
        self.head = lax.axis_index("head")
        self.core = lax.rem(ctx, 2)
        self.phys_y = lax.rem(ctx // 2, self.ny)
        self.phys_x = ctx // (2 * self.ny)
        self.y = self.ny - 1 - self.phys_y if reverse else self.phys_y
        self.x = self.nx - 1 - self.phys_x if reverse else self.phys_x
        self.order = 1 - self.core if reverse else self.core

    def device(self, x, y, core):
        return ((x * self.ny + y) * 2 + core, self.head)

    def partner(self):
        return self.device(self.phys_x, self.phys_y, 1 - self.core)

    def along_y(self, y):
        return self.device(self.phys_x, self.ny - 1 - y if self.reverse else y, self.core)

    def along_x(self, x):
        return self.device(self.nx - 1 - x if self.reverse else x, self.phys_y, self.core)


class Scan:
    def __init__(self, way, place, rate, lengths, refs, pending):
        self.way, self.place, self.rate, self.lengths = way, place, rate, lengths
        (self.loc, self.pair, self.csend, self.a1, self.tx, self.psend, self.a2, self.fsend, self.st) = refs[:9]
        (self.c_s, self.c_r, self.a1_s, self.a1_r, self.x_s, self.x_r, self.a2_s, self.a2_r, self.f_s, self.f_r) = refs[9:]
        self.pending = pending
        self.heads = self.loc.shape[2]
        self.rows = self.csend.shape[4]
        self.half = self.fsend.shape[3]
        self.name = ("fwd", "bwd")[way]

    def decay(self, h, tokens):
        return jnp.exp(jnp.full((1, 128), -self.rate[h], F32) * tokens)

    def copy(self, src, dst, send, recv, device):
        return pltpu.make_async_remote_copy(
            src_ref=src, dst_ref=dst, send_sem=send, recv_sem=recv, device_id=device, device_id_type=MESH
        )

    def start(self, copy):
        copy.start()
        self.pending.append(copy)

    def half_of(self, core):
        return pl.ds(pl.multiple_of(core * self.half, self.half), self.half)

    def pair_copy(self, s):
        w, p = self.way, self.place
        src = self.loc.at[w, s, :, self.half_of(1 - p.core), :]
        return self.copy(src, self.pair.at[w, s], self.c_s.at[w, s], self.c_r.at[w, s], p.partner())

    def start_pair(self, s):
        self.start(self.pair_copy(s))

    def first_second(self, s, h):
        own = self.loc[self.way, s, h, self.half_of(self.place.core), :]
        other = self.pair[self.way, s, h]
        leads = self.place.order == 0
        return jnp.where(leads, own, other), jnp.where(leads, other, own)

    def send_along_y(self, src, dst, send, recv, s):
        w, p = self.way, self.place
        for k in far_first(p.ny):
            to = lax.rem(p.y + k, p.ny)
            self.start(self.copy(src.at[w, s, to], dst.at[w, s, p.y], send.at[w, s, k], recv.at[w, s, p.y], p.along_y(to)))

    def wait_along(self, buf, sem, here, n, s, device):
        w = self.way
        for k in range(1, n):
            at = lax.rem(here + k, n)
            landed = buf.at[w, s, at]
            self.copy(landed, landed, sem.at[w, s, at], sem.at[w, s, at], device(at)).wait_recv()

    def chip(self, s):
        w, p = self.way, self.place
        with jax.named_scope(f"{self.name}_pair{s}"):
            self.pair_copy(s).wait_recv()
        for h in range(self.heads):
            first, second = self.first_second(s, h)
            both = self.decay(h, float(self.lengths[s])) * first + second
            for j in range(p.ny):
                self.csend[w, s, j, h] = both[j * self.rows : (j + 1) * self.rows]
        self.a1[w, s, p.y] = self.csend[w, s, p.y]
        self.send_along_y(self.csend, self.a1, self.a1_s, self.a1_r, s)

    def column(self, s):
        w, p = self.way, self.place
        with jax.named_scope(f"{self.name}_gather{s}"):
            self.wait_along(self.a1, self.a1_r, p.y, p.ny, s, p.along_y)
        for h in range(self.heads):
            step = self.decay(h, 2.0 * self.lengths[s])
            total = self.a1[w, s, 0, h]
            for j in range(1, p.ny):
                total = step * total + self.a1[w, s, j, h]
            self.tx[w, s, p.x, h] = total
        for k in far_first(p.nx):
            to = lax.rem(p.x + k, p.nx)
            mine = self.tx.at[w, s, p.x]
            self.start(self.copy(mine, mine, self.x_s.at[w, s, k], self.x_r.at[w, s, p.x], p.along_x(to)))

    def columns(self, s):
        w, p = self.way, self.place
        with jax.named_scope(f"{self.name}_x{s}"):
            self.wait_along(self.tx, self.x_r, p.x, p.nx, s, p.along_x)
        bases, totals = [], []
        for h in range(self.heads):
            step = self.decay(h, 2.0 * self.lengths[s] * p.ny)
            run = self.tx[w, s, 0, h]
            base = jnp.zeros_like(run)
            for j in range(1, p.nx):
                base = jnp.where(p.x == j, run, base)
                run = step * run + self.tx[w, s, j, h]
            bases.append(base)
            totals.append(run)
        return bases, totals

    def spread(self, s, bases, given):
        w, p = self.way, self.place
        for h in range(self.heads):
            step = self.decay(h, 2.0 * self.lengths[s])
            entry = bases[h]
            if given is not None:
                before = (p.x * (2 * p.ny * self.lengths[s])).astype(F32)
                entry = entry + self.decay(h, before) * given[h]
            for j in range(p.ny):
                self.psend[w, s, j, h] = entry
                if j < p.ny - 1:
                    entry = step * entry + self.a1[w, s, j, h]
        self.a2[w, s, p.y] = self.psend[w, s, p.y]
        self.send_along_y(self.psend, self.a2, self.a2_s, self.a2_r, s)

    def final_copy(self, s):
        w, p = self.way, self.place
        dst = self.st.at[w, s, :, self.half_of(p.core), :]
        return self.copy(self.fsend.at[w, s], dst, self.f_s.at[w, s], self.f_r.at[w, s], p.partner())

    def finish(self, s):
        w, p = self.way, self.place
        with jax.named_scope(f"{self.name}_spread{s}"):
            self.wait_along(self.a2, self.a2_r, p.y, p.ny, s, p.along_y)
        leads = p.order == 0
        for h in range(self.heads):
            entry = jnp.concatenate([self.a2[w, s, j, h] for j in range(p.ny)], axis=0)
            first, _ = self.first_second(s, h)
            after = self.decay(h, float(self.lengths[s])) * entry + first
            self.st[w, s, h, self.half_of(p.core), :] = jnp.where(leads, entry, after)
            self.fsend[w, s, h] = jnp.where(leads, after, entry)
        self.start(self.final_copy(s))

    def ready(self, s):
        w, p = self.way, self.place
        landed = self.st.at[w, s, :, self.half_of(1 - p.core), :]
        with jax.named_scope(f"{self.name}_last{s}"):
            self.copy(landed, landed, self.f_r.at[w, s], self.f_r.at[w, s], p.partner()).wait_recv()


def far_first(n):
    return sorted(range(1, n), key=lambda k: -min(k, n - k))


def column_of(row):
    return jnp.broadcast_to(row, (128, 128)).T


def kernel(
    grid, nz, *refs
):
    places = refs[:10]
    py, ry, pdq, pdk, pdv, rdq, rdk, rdv = refs[10:18]
    held = refs[18:28]
    rate, gain, pq, pk, pv, pc, rq, rk, rv, rc = held
    loc, pair, csend, a1, tx, psend, a2, fsend, st, stat, pmix, rmix, pout, rout, pgrad, rgrad, dk_p, dv_p, dk_r, dv_r = refs[28:48]
    in_s, c_s, c_r, a1_s, a1_r, x_s, x_r, a2_s, a2_r, f_s, f_r, z_s, z_r = refs[48:]
    loads = {id(dst): pltpu.make_async_copy(src, dst, in_s.at[i]) for i, (src, dst) in enumerate(zip(places, held))}
    for ref in (rate, pk, pv, rk, rv, gain, pq, rq, pc, rc):
        loads[id(ref)].start()

    def arrive(*wanted):
        for ref in wanted:
            loads[id(ref)].wait()

    heads, tokens, width = pq.shape
    count = rq.shape[2]
    features = float(heads * nz * width)
    ahead, back = Place(grid, False), Place(grid, True)
    ctx, z = lax.axis_index("ctx"), ahead.head

    barrier = pltpu.get_barrier_semaphore()
    peers = [ahead.partner()]
    peers += [ahead.along_y(lax.rem(ahead.y + k, grid[1])) for k in range(1, grid[1])]
    peers += [ahead.along_x(lax.rem(ahead.x + k, grid[0])) for k in range(1, grid[0])]
    peers += [(ctx, lax.rem(z + k, nz)) for k in range(1, nz)]
    for peer in peers:
        pl.semaphore_signal(barrier, inc=1, device_id=peer, device_id_type=MESH)

    pending = []
    refs = (loc, pair, csend, a1, tx, psend, a2, fsend, st, c_s, c_r, a1_s, a1_r, x_s, x_r, a2_s, a2_r, f_s, f_r)
    lengths = (tokens, count, count)
    fwd = Scan(0, ahead, rate, lengths, refs, pending)
    bwd = Scan(1, back, rate, lengths, refs, pending)

    row = lax.broadcasted_iota(jnp.int32, (128, 128), 0)
    col = lax.broadcasted_iota(jnp.int32, (128, 128), 1)
    lag = (row - col).astype(F32)
    causal = row >= col
    apart = (row // count) != (col // count)
    place_p = row.astype(F32)
    place_r = lax.rem(row, count).astype(F32)

    def power(h, steps):
        return jnp.exp(jnp.full((128, 128), -rate[h], F32) * steps)

    def pairs(ref, h):
        return jnp.concatenate([ref[0, h], ref[1, h]], axis=0)

    def masks(h):
        mask = jnp.where(causal, power(h, jnp.maximum(lag, 0.0)), 0.0)
        return mask, jnp.where(apart, 0.0, mask)

    def fwd_states(s):
        for h in range(heads):
            if s == 0:
                keys = (pk[h].astype(F32) * power(h, tokens - 1.0 - place_p)).astype(BF16)
                loc[0, 0, h] = dot_tn(keys, pv[h])
            else:
                keys = (rk[s - 1, h].astype(F32) * power(h, count - 1.0 - place_p)[:count]).astype(BF16)
                loc[0, s, h] = dot_tn(keys, rv[s - 1, h])

    with jax.named_scope("local_p"):
        arrive(rate, pk, pv)
        fwd_states(0)
    with jax.named_scope("entry"):
        pl.semaphore_wait(barrier, len(peers))
    fwd.start_pair(0)
    with jax.named_scope("local_r"):
        arrive(rk, rv)
        fwd_states(1)
        fwd.start_pair(1)
        fwd_states(2)
        fwd.start_pair(2)
    for s in range(3):
        fwd.chip(s)

    with jax.named_scope("intra"):
        arrive(pq, rq)
        for h in range(heads):
            mask_p, mask_r = masks(h)
            pmix[h] = (dot_nt(pq[h], pk[h]) * mask_p).astype(BF16)
            rmix[h] = (dot_nt(pairs(rq, h), pairs(rk, h)) * mask_r).astype(BF16)
            pout[h] = dot_nn(pmix[h], pv[h])
            rout[h] = dot_nn(rmix[h], pairs(rv, h))

    arrive(gain, pc, rc)
    fwd.column(0)
    fwd.column(1)
    bases, final = fwd.columns(0)
    fwd.spread(0, bases, None)
    fwd.column(2)
    for s in (1, 2):
        bases, _ = fwd.columns(s)
        fwd.spread(s, bases, final)

    def outputs(s):
        fwd.ready(s)
        rows = tokens if s == 0 else count
        part = slice(0, rows) if s == 0 else slice((s - 1) * count, s * count)
        squares, inner = jnp.zeros((rows, 128), F32), jnp.zeros((rows, 128), F32)
        for h in range(heads):
            buf = pout if s == 0 else rout
            queries, cot = (pq[h], pc[h]) if s == 0 else (rq[s - 1, h], rc[s - 1, h])
            across = dot_nn(queries, st[0, s, h].astype(BF16))
            out = buf[h, part, :] + power(h, place_p + 1.0)[:rows] * across
            buf[h, part, :] = out
            squares += out * out
            inner += gain[h : h + 1] * cot.astype(F32) * out
        both = [squares, inner] if s == 0 else [jnp.concatenate([squares, inner], axis=0)]
        lines = [jnp.sum(a.T, axis=0, keepdims=True) for a in both]
        stat[s, z] = jnp.concatenate(lines + [jnp.zeros((8 - len(lines), 128), F32)], axis=0)
        for k in far_first(nz):
            to = (ctx, lax.rem(z + k, nz))
            fwd.start(fwd.copy(stat.at[s, z], stat.at[s, z], z_s.at[s, k], z_r.at[s, z], to))

    def norms(s):
        with jax.named_scope(f"norm{s}"):
            for k in range(1, nz):
                at = lax.rem(z + k, nz)
                landed = stat.at[s, at]
                fwd.copy(landed, landed, z_r.at[s, at], z_r.at[s, at], (ctx, at)).wait_recv()
        total = stat[s, 0]
        for k in range(1, nz):
            total = total + stat[s, k]
        if s == 0:
            inv = lax.rsqrt(total[0:1] / features + 1e-05)
            return column_of(inv), column_of(total[1:2] * inv * inv * inv / features)
        both = column_of(total[0:1])
        inv = lax.rsqrt(both[:count] / features + 1e-05)
        return inv, both[count:] * inv * inv * inv / features

    def gradients(s):
        inv, coef = norms(s)
        rows = tokens if s == 0 else count
        part = slice(0, rows) if s == 0 else slice((s - 1) * count, s * count)
        for h in range(heads):
            out = (pout if s == 0 else rout)[h, part, :]
            queries, cot = (pq[h], pc[h]) if s == 0 else (rq[s - 1, h], rc[s - 1, h])
            grad = (gain[h : h + 1] * cot.astype(F32) * inv - out * coef).astype(BF16)
            if s == 0:
                pgrad[h] = grad
            else:
                rgrad[h, part, :] = grad
            queries = (queries.astype(F32) * power(h, place_p + 1.0)[:rows]).astype(BF16)
            loc[1, s, h] = dot_tn(queries, grad)
        bwd.start_pair(s)
        return inv

    def normed(s, inv):
        for h in range(heads):
            if s == 0:
                py[h] = (gain[h : h + 1] * pout[h] * inv).astype(BF16)
            else:
                ry[s - 1, h] = (gain[h : h + 1] * rout[h, (s - 1) * count : s * count, :] * inv).astype(BF16)

    fwd.finish(0)
    fwd.finish(1)
    outputs(0)
    fwd.finish(2)
    outputs(1)
    outputs(2)
    inv_p = gradients(0)
    inv_0 = gradients(1)
    bwd.chip(0)
    inv_1 = gradients(2)
    bwd.chip(1)
    bwd.chip(2)

    with jax.named_scope("inner"):
        for s, inv in enumerate((inv_p, inv_0, inv_1)):
            normed(s, inv)
        for h in range(heads):
            mask_p, mask_r = masks(h)
            grad = pgrad[h]
            dmix = (dot_nt(grad, pv[h]) * mask_p).astype(BF16)
            across = dot_nt(grad, st[0, 0, h].astype(BF16))
            pdq[h] = (dot_nn(dmix, pk[h]) + power(h, place_p + 1.0) * across).astype(BF16)
            dk_p[h] = dot_tn(dmix, pq[h])
            dv_p[h] = dot_tn(pmix[h], grad)
            grad = rgrad[h]
            dmix = (dot_nt(grad, pairs(rv, h)) * mask_r).astype(BF16)
            across = [dot_nt(grad[r * count : (r + 1) * count], st[0, 1 + r, h].astype(BF16)) for r in range(2)]
            queries = dot_nn(dmix, pairs(rk, h)) + power(h, place_r + 1.0) * jnp.concatenate(across, axis=0)
            dk_r[h] = dot_tn(dmix, pairs(rq, h))
            dv_r[h] = dot_tn(rmix[h], grad)
            for r in range(2):
                rdq[r, h] = queries[r * count : (r + 1) * count].astype(BF16)

    bwd.column(0)
    bwd.column(1)
    bwd.column(2)
    given = [0.0] * heads
    for s in (1, 2):
        bases, totals = bwd.columns(s)
        bwd.spread(s, bases, None)
        given = [a + b for a, b in zip(given, totals)]
    bases, _ = bwd.columns(0)
    bwd.spread(0, bases, given)

    def responses(r):
        bwd.ready(1 + r)
        part = slice(r * count, (r + 1) * count)
        for h in range(heads):
            later = st[1, 1 + r, h].astype(BF16)
            fade = power(h, count - 1.0 - place_p)[:count]
            rdk[r, h] = (dk_r[h, part, :] + fade * dot_nt(rv[r, h], later)).astype(BF16)
            rdv[r, h] = (dv_r[h, part, :] + fade * dot_nn(rk[r, h], later)).astype(BF16)

    bwd.finish(1)
    bwd.finish(2)
    responses(0)
    bwd.finish(0)
    responses(1)
    bwd.ready(0)
    with jax.named_scope("end"):
        for h in range(heads):
            later = st[1, 0, h].astype(BF16)
            fade = power(h, tokens - 1.0 - place_p)
            pdk[h] = (dk_p[h] + fade * dot_nt(pv[h], later)).astype(BF16)
            pdv[h] = (dv_p[h] + fade * dot_nn(pk[h], later)).astype(BF16)
        for copy in pending:
            copy.wait_send()


def hand_over(*refs):
    copies = [pltpu.make_async_copy(src, dst, refs[16].at[i]) for i, (src, dst) in enumerate(zip(refs[:8], refs[8:16]))]
    for copy in copies:
        copy.start()
    for copy in copies:
        copy.wait()


def shards(grid, nz, prompt_q, prompt_k, prompt_v, resp_q, resp_k, resp_v, decay_rate, norm_gain, prompt_cot, resp_cot):
    nx, ny, _ = grid
    tokens, heads, width = prompt_q.shape
    count = resp_q.shape[1]
    half, rows = width // 2, width // 2 // ny
    prompt = [jnp.transpose(a, (1, 0, 2)) for a in (prompt_q, prompt_k, prompt_v, prompt_cot)]
    resp = [jnp.transpose(a, (0, 2, 1, 3)) for a in (resp_q, resp_k, resp_v, resp_cot)]
    flat = pltpu.VMEM((heads, tokens, width), BF16)
    duo = pltpu.VMEM((2, heads, count, width), BF16)
    vmem, hbm = pl.BlockSpec(memory_space=pltpu.VMEM), pl.BlockSpec(memory_space=pltpu.HBM)
    block = (heads, tokens, width)
    scratch = [pltpu.SMEM((heads,), F32), pltpu.VMEM((heads, width), F32)]
    scratch += [pltpu.VMEM(block, BF16)] * 4 + [pltpu.VMEM((2, heads, count, width), BF16)] * 4
    scratch += [
        pltpu.VMEM((2, 3, heads, width, width), F32),
        pltpu.VMEM((2, 3, heads, half, width), F32),
        pltpu.VMEM((2, 3, ny, heads, rows, width), F32),
        pltpu.VMEM((2, 3, ny, heads, rows, width), F32),
        pltpu.VMEM((2, 3, nx, heads, rows, width), F32),
        pltpu.VMEM((2, 3, ny, heads, rows, width), F32),
        pltpu.VMEM((2, 3, ny, heads, rows, width), F32),
        pltpu.VMEM((2, 3, heads, half, width), F32),
        pltpu.VMEM((2, 3, heads, width, width), F32),
        pltpu.VMEM((3, nz, 8, width), F32),
        pltpu.VMEM(block, BF16),
        pltpu.VMEM(block, BF16),
        pltpu.VMEM(block, F32),
        pltpu.VMEM(block, F32),
        pltpu.VMEM(block, BF16),
        pltpu.VMEM(block, BF16),
        pltpu.VMEM(block, F32),
        pltpu.VMEM(block, F32),
        pltpu.VMEM(block, F32),
        pltpu.VMEM(block, F32),
    ]
    dma = pltpu.SemaphoreType.DMA
    scratch += [dma((10,))] + [dma((2, 3))] * 2 + [dma((2, 3, ny))] * 2 + [dma((2, 3, nx))] * 2
    scratch += [dma((2, 3, ny))] * 2 + [dma((2, 3))] * 2 + [dma((3, nz))] * 2
    out = pl.pallas_call(
        functools.partial(kernel, grid, nz),
        out_shape=(flat, duo, flat, flat, flat, duo, duo, duo),
        in_specs=[hbm] * 10,
        out_specs=(vmem,) * 8,
        scratch_shapes=scratch,
        compiler_params=pltpu.CompilerParams(collective_id=0, has_side_effects=True, vmem_limit_bytes=40 << 20),
    )(*(pltpu.with_memory_space_constraint(a, pltpu.HBM) for a in (decay_rate, norm_gain, *prompt, *resp)))
    out = pl.pallas_call(
        hand_over,
        out_shape=tuple(jax.ShapeDtypeStruct(a.shape, a.dtype) for a in out),
        in_specs=[vmem] * 8,
        out_specs=(hbm,) * 8,
        scratch_shapes=[dma((8,))],
        compiler_params=pltpu.CompilerParams(vmem_limit_bytes=8 << 20),
    )(*out)
    return tuple(
        jnp.transpose(a, (1, 0, 2)) if a.ndim == 3 else jnp.transpose(a, (0, 2, 1, 3)) for a in out
    )


def solution(mesh):
    flat, duo = P("ctx", "head", None), P(None, "ctx", "head", None)
    return jax.shard_map(
        functools.partial(shards, GRID, mesh.shape["head"]),
        mesh=mesh,
        in_specs=(flat, flat, flat, duo, duo, duo, P("head"), P("head", None), flat, duo),
        out_specs=(flat, duo, flat, flat, flat, duo, duo, duo),
        check_vma=False,
    )
```

```python
import functools

import jax
import jax.numpy as jnp
from jax import lax
from jax.experimental import pallas as pl
from jax.experimental.pallas import tpu as pltpu
from jax.sharding import PartitionSpec as P

GRID = (4, 8, 2)
MESH = pl.DeviceIdType.MESH
F32 = jnp.float32
BF16 = jnp.bfloat16


def dot(left, right, dims):
    return lax.dot_general(left, right, (dims, ((), ())), preferred_element_type=F32)


def dot_nn(left, right):
    return dot(left, right, ((1,), (0,)))


def dot_nt(left, right):
    return dot(left, right, ((1,), (1,)))


def dot_tn(left, right):
    return dot(left, right, ((0,), (0,)))


class Place:
    def __init__(self, grid, reverse):
        self.nx, self.ny, _ = grid
        self.reverse = reverse
        ctx = lax.axis_index("ctx")
        self.head = lax.axis_index("head")
        self.core = lax.rem(ctx, 2)
        self.phys_y = lax.rem(ctx // 2, self.ny)
        self.phys_x = ctx // (2 * self.ny)
        self.y = self.ny - 1 - self.phys_y if reverse else self.phys_y
        self.x = self.nx - 1 - self.phys_x if reverse else self.phys_x
        self.order = 1 - self.core if reverse else self.core

    def device(self, x, y, core):
        return ((x * self.ny + y) * 2 + core, self.head)

    def partner(self):
        return self.device(self.phys_x, self.phys_y, 1 - self.core)

    def along_y(self, y):
        return self.device(self.phys_x, self.ny - 1 - y if self.reverse else y, self.core)

    def along_x(self, x):
        return self.device(self.nx - 1 - x if self.reverse else x, self.phys_y, self.core)


class Scan:
    def __init__(self, way, place, rate, lengths, refs):
        self.way, self.place, self.rate, self.lengths = way, place, rate, lengths
        (self.loc, self.pair, self.csend, self.a1, self.tx, self.psend, self.a2, self.fsend, self.st) = refs[:9]
        (self.c_s, self.c_r, self.a1_s, self.a1_r, self.x_s, self.x_r, self.a2_s, self.a2_r, self.f_s, self.f_r) = refs[9:]
        self.heads = self.loc.shape[2]
        self.rows = self.csend.shape[4]
        self.half = self.fsend.shape[3]
        self.name = ("fwd", "bwd")[way]

    def decay(self, h, tokens):
        return jnp.exp(jnp.full((1, 128), -self.rate[h], F32) * tokens)

    def copy(self, src, dst, send, recv, device):
        return pltpu.make_async_remote_copy(
            src_ref=src, dst_ref=dst, send_sem=send, recv_sem=recv, device_id=device, device_id_type=MESH
        )

    def half_of(self, core):
        return pl.ds(pl.multiple_of(core * self.half, self.half), self.half)

    def pair_copy(self, s):
        w, p = self.way, self.place
        src = self.loc.at[w, s, :, self.half_of(1 - p.core), :]
        return self.copy(src, self.pair.at[w, s], self.c_s, self.c_r.at[w, s], p.partner())

    def start_pair(self, s):
        self.pair_copy(s).start()

    def first_second(self, s, h):
        own = self.loc[self.way, s, h, self.half_of(self.place.core), :]
        other = self.pair[self.way, s, h]
        leads = self.place.order == 0
        return jnp.where(leads, own, other), jnp.where(leads, other, own)

    def send_along_y(self, src, dst, send, recv, s):
        w, p = self.way, self.place
        for k in far_first(p.ny):
            to = lax.rem(p.y + k, p.ny)
            self.copy(src.at[w, s, to], dst.at[w, s, p.y], send, recv.at[w, s], p.along_y(to)).start()

    def wait_all(self, buf, sem, s):
        others = buf.at[self.way, s, pl.ds(0, buf.shape[2] - 1)]
        self.copy(others, others, sem.at[self.way, s], sem.at[self.way, s], self.place.partner()).wait_recv()

    def chip(self, s):
        w, p = self.way, self.place
        with jax.named_scope(f"{self.name}_pair{s}"):
            self.pair_copy(s).wait_recv()
        for h in range(self.heads):
            first, second = self.first_second(s, h)
            both = self.decay(h, float(self.lengths[s])) * first + second
            for j in range(p.ny):
                self.csend[w, s, j, h] = both[j * self.rows : (j + 1) * self.rows]
        self.a1[w, s, p.y] = self.csend[w, s, p.y]
        self.send_along_y(self.csend, self.a1, self.a1_s, self.a1_r, s)

    def column(self, s):
        w, p = self.way, self.place
        with jax.named_scope(f"{self.name}_gather{s}"):
            self.wait_all(self.a1, self.a1_r, s)
        for h in range(self.heads):
            step = self.decay(h, 2.0 * self.lengths[s])
            total = self.a1[w, s, 0, h]
            for j in range(1, p.ny):
                total = step * total + self.a1[w, s, j, h]
            self.tx[w, s, p.x, h] = total
        for k in far_first(p.nx):
            to = lax.rem(p.x + k, p.nx)
            mine = self.tx.at[w, s, p.x]
            self.copy(mine, mine, self.x_s, self.x_r.at[w, s], p.along_x(to)).start()

    def columns(self, s):
        w, p = self.way, self.place
        with jax.named_scope(f"{self.name}_x{s}"):
            self.wait_all(self.tx, self.x_r, s)
        bases, totals = [], []
        for h in range(self.heads):
            step = self.decay(h, 2.0 * self.lengths[s] * p.ny)
            run = self.tx[w, s, 0, h]
            base = jnp.zeros_like(run)
            for j in range(1, p.nx):
                base = jnp.where(p.x == j, run, base)
                run = step * run + self.tx[w, s, j, h]
            bases.append(base)
            totals.append(run)
        return bases, totals

    def spread(self, s, bases, given):
        w, p = self.way, self.place
        for h in range(self.heads):
            step = self.decay(h, 2.0 * self.lengths[s])
            entry = bases[h]
            if given is not None:
                before = (p.x * (2 * p.ny * self.lengths[s])).astype(F32)
                entry = entry + self.decay(h, before) * given[h]
            for j in range(p.ny):
                self.psend[w, s, j, h] = entry
                if j < p.ny - 1:
                    entry = step * entry + self.a1[w, s, j, h]
        self.a2[w, s, p.y] = self.psend[w, s, p.y]
        self.send_along_y(self.psend, self.a2, self.a2_s, self.a2_r, s)

    def final_copy(self, s):
        w, p = self.way, self.place
        dst = self.st.at[w, s, :, self.half_of(p.core), :]
        return self.copy(self.fsend.at[w, s], dst, self.f_s, self.f_r.at[w, s], p.partner())

    def finish(self, s):
        w, p = self.way, self.place
        with jax.named_scope(f"{self.name}_spread{s}"):
            self.wait_all(self.a2, self.a2_r, s)
        leads = p.order == 0
        for h in range(self.heads):
            entry = jnp.concatenate([self.a2[w, s, j, h] for j in range(p.ny)], axis=0)
            first, _ = self.first_second(s, h)
            after = self.decay(h, float(self.lengths[s])) * entry + first
            self.st[w, s, h, self.half_of(p.core), :] = jnp.where(leads, entry, after)
            self.fsend[w, s, h] = jnp.where(leads, after, entry)
        self.final_copy(s).start()

    def ready(self, s):
        w, p = self.way, self.place
        landed = self.st.at[w, s, :, self.half_of(1 - p.core), :]
        with jax.named_scope(f"{self.name}_last{s}"):
            self.copy(landed, landed, self.f_r.at[w, s], self.f_r.at[w, s], p.partner()).wait_recv()


def far_first(n):
    return sorted(range(1, n), key=lambda k: -min(k, n - k))


def reaching(n):
    strides, reach = [], 1
    while reach < n // 2:
        strides.append(min(reach, n // 2 - reach))
        reach += strides[-1]
    return strides


def column_of(row):
    return jnp.broadcast_to(row, (128, 128)).T


def kernel(
    grid, nz, *refs
):
    places = refs[:10]
    py, ry, pdq, pdk, pdv, rdq, rdk, rdv = refs[10:18]
    held = refs[18:28]
    rate, gain, pq, pk, pv, pc, rq, rk, rv, rc = held
    loc, pair, csend, a1, tx, psend, a2, fsend, st, stat, pmix, rmix, pout, rout, pgrad, rgrad, dk_p, dv_p, dk_r, dv_r = refs[28:48]
    in_s, c_s, c_r, a1_s, a1_r, x_s, x_r, a2_s, a2_r, f_s, f_r, z_s, z_r, told = refs[48:]
    loads = {id(dst): pltpu.make_async_copy(src, dst, in_s.at[i]) for i, (src, dst) in enumerate(zip(places, held))}
    for ref in (rate, pk, pv, rk, rv, gain, pq, rq, pc, rc):
        loads[id(ref)].start()

    def arrive(*wanted):
        for ref in wanted:
            loads[id(ref)].wait()

    heads, tokens, width = pq.shape
    count = rq.shape[2]
    features = float(heads * nz * width)
    ahead, back = Place(grid, False), Place(grid, True)
    ctx, z = lax.axis_index("ctx"), ahead.head

    barrier = pltpu.get_barrier_semaphore()
    peers = [ahead.partner()]
    peers += [ahead.along_y(lax.rem(ahead.y + k, grid[1])) for k in range(1, grid[1])]
    peers += [ahead.along_x(lax.rem(ahead.x + k, grid[0])) for k in range(1, grid[0])]
    peers += [(ctx, lax.rem(z + 1, nz)), (ctx, lax.rem(z + nz - 1, nz))]
    for peer in peers:
        pl.semaphore_signal(barrier, inc=1, device_id=peer, device_id_type=MESH)

    refs = (loc, pair, csend, a1, tx, psend, a2, fsend, st, c_s, c_r, a1_s, a1_r, x_s, x_r, a2_s, a2_r, f_s, f_r)
    lengths = (tokens, count, count)
    fwd = Scan(0, ahead, rate, lengths, refs)
    bwd = Scan(1, back, rate, lengths, refs)

    row = lax.broadcasted_iota(jnp.int32, (128, 128), 0)
    col = lax.broadcasted_iota(jnp.int32, (128, 128), 1)
    lag = (row - col).astype(F32)
    causal = row >= col
    apart = (row // count) != (col // count)
    place_p = row.astype(F32)
    place_r = lax.rem(row, count).astype(F32)

    def power(h, steps):
        return jnp.exp(jnp.full((128, 128), -rate[h], F32) * steps)

    def pairs(ref, h):
        return jnp.concatenate([ref[0, h], ref[1, h]], axis=0)

    def masks(h):
        mask = jnp.where(causal, power(h, jnp.maximum(lag, 0.0)), 0.0)
        return mask, jnp.where(apart, 0.0, mask)

    strides = reaching(nz)

    def tell(i):
        for side, stride in enumerate((strides[i], nz - strides[i])):
            to = (ctx, lax.rem(z + stride, nz))
            pl.semaphore_signal(told.at[i, side], inc=1, device_id=to, device_id_type=MESH)

    def hear(i):
        with jax.named_scope(f"hear{i}"):
            for side in range(2):
                pl.semaphore_wait(told.at[i, side], 1)
        if i + 1 < len(strides):
            tell(i + 1)

    def fwd_states(s):
        for h in range(heads):
            if s == 0:
                keys = (pk[h].astype(F32) * power(h, tokens - 1.0 - place_p)).astype(BF16)
                loc[0, 0, h] = dot_tn(keys, pv[h])
            else:
                keys = (rk[s - 1, h].astype(F32) * power(h, count - 1.0 - place_p)[:count]).astype(BF16)
                loc[0, s, h] = dot_tn(keys, rv[s - 1, h])

    with jax.named_scope("local_p"):
        arrive(rate, pk, pv)
        fwd_states(0)
    with jax.named_scope("entry"):
        pl.semaphore_wait(barrier, len(peers))
    fwd.start_pair(0)
    if strides:
        tell(0)
    with jax.named_scope("local_r"):
        arrive(rk, rv)
        fwd_states(1)
        fwd.start_pair(1)
        fwd_states(2)
        fwd.start_pair(2)
    for s in range(3):
        fwd.chip(s)
    if strides:
        hear(0)

    with jax.named_scope("intra"):
        arrive(pq, rq)
        for h in range(heads):
            mask_p, mask_r = masks(h)
            pmix[h] = (dot_nt(pq[h], pk[h]) * mask_p).astype(BF16)
            rmix[h] = (dot_nt(pairs(rq, h), pairs(rk, h)) * mask_r).astype(BF16)
            pout[h] = dot_nn(pmix[h], pv[h])
            rout[h] = dot_nn(rmix[h], pairs(rv, h))

    arrive(gain, pc, rc)
    if len(strides) > 1:
        hear(1)
    fwd.column(0)
    for i in range(2, len(strides)):
        hear(i)
    fwd.column(1)
    bases, final = fwd.columns(0)
    fwd.spread(0, bases, None)
    fwd.column(2)
    for s in (1, 2):
        bases, _ = fwd.columns(s)
        fwd.spread(s, bases, final)

    def outputs(s):
        fwd.ready(s)
        rows = tokens if s == 0 else count
        part = slice(0, rows) if s == 0 else slice((s - 1) * count, s * count)
        squares, inner = jnp.zeros((rows, 128), F32), jnp.zeros((rows, 128), F32)
        for h in range(heads):
            buf = pout if s == 0 else rout
            queries, cot = (pq[h], pc[h]) if s == 0 else (rq[s - 1, h], rc[s - 1, h])
            across = dot_nn(queries, st[0, s, h].astype(BF16))
            out = buf[h, part, :] + power(h, place_p + 1.0)[:rows] * across
            buf[h, part, :] = out
            squares += out * out
            inner += gain[h : h + 1] * cot.astype(F32) * out
        both = [squares, inner] if s == 0 else [jnp.concatenate([squares, inner], axis=0)]
        lines = [jnp.sum(a.T, axis=0, keepdims=True) for a in both]
        stat[s, z] = jnp.concatenate(lines + [jnp.zeros((8 - len(lines), 128), F32)], axis=0)
        for k in far_first(nz):
            to = (ctx, lax.rem(z + k, nz))
            fwd.copy(stat.at[s, z], stat.at[s, z], z_s, z_r.at[s], to).start()

    def norms(s):
        with jax.named_scope(f"norm{s}"):
            others = stat.at[s, pl.ds(0, nz - 1)]
            fwd.copy(others, others, z_r.at[s], z_r.at[s], ahead.partner()).wait_recv()
        total = stat[s, 0]
        for k in range(1, nz):
            total = total + stat[s, k]
        if s == 0:
            inv = lax.rsqrt(total[0:1] / features + 1e-05)
            return column_of(inv), column_of(total[1:2] * inv * inv * inv / features)
        both = column_of(total[0:1])
        inv = lax.rsqrt(both[:count] / features + 1e-05)
        return inv, both[count:] * inv * inv * inv / features

    def gradients(s):
        inv, coef = norms(s)
        rows = tokens if s == 0 else count
        part = slice(0, rows) if s == 0 else slice((s - 1) * count, s * count)
        for h in range(heads):
            out = (pout if s == 0 else rout)[h, part, :]
            queries, cot = (pq[h], pc[h]) if s == 0 else (rq[s - 1, h], rc[s - 1, h])
            grad = (gain[h : h + 1] * cot.astype(F32) * inv - out * coef).astype(BF16)
            if s == 0:
                pgrad[h] = grad
            else:
                rgrad[h, part, :] = grad
            queries = (queries.astype(F32) * power(h, place_p + 1.0)[:rows]).astype(BF16)
            loc[1, s, h] = dot_tn(queries, grad)
        bwd.start_pair(s)
        return inv

    def normed(s, inv):
        for h in range(heads):
            if s == 0:
                py[h] = (gain[h : h + 1] * pout[h] * inv).astype(BF16)
            else:
                ry[s - 1, h] = (gain[h : h + 1] * rout[h, (s - 1) * count : s * count, :] * inv).astype(BF16)

    for s in range(3):
        fwd.finish(s)
        outputs(s)
    scales = []
    for s in range(3):
        scales.append(gradients(s))
        bwd.chip(s)

    with jax.named_scope("inner"):
        for s, inv in enumerate(scales):
            normed(s, inv)
        for h in range(heads):
            mask_p, mask_r = masks(h)
            grad = pgrad[h]
            dmix = (dot_nt(grad, pv[h]) * mask_p).astype(BF16)
            across = dot_nt(grad, st[0, 0, h].astype(BF16))
            pdq[h] = (dot_nn(dmix, pk[h]) + power(h, place_p + 1.0) * across).astype(BF16)
            dk_p[h] = dot_tn(dmix, pq[h])
            dv_p[h] = dot_tn(pmix[h], grad)
            grad = rgrad[h]
            dmix = (dot_nt(grad, pairs(rv, h)) * mask_r).astype(BF16)
            across = [dot_nt(grad[r * count : (r + 1) * count], st[0, 1 + r, h].astype(BF16)) for r in range(2)]
            queries = dot_nn(dmix, pairs(rk, h)) + power(h, place_r + 1.0) * jnp.concatenate(across, axis=0)
            dk_r[h] = dot_tn(dmix, pairs(rq, h))
            dv_r[h] = dot_tn(rmix[h], grad)
            for r in range(2):
                rdq[r, h] = queries[r * count : (r + 1) * count].astype(BF16)

    bwd.column(0)
    bwd.column(1)
    bwd.column(2)
    given = [0.0] * heads
    for s in (1, 2):
        bases, totals = bwd.columns(s)
        bwd.spread(s, bases, None)
        given = [a + b for a, b in zip(given, totals)]
    bases, _ = bwd.columns(0)
    bwd.spread(0, bases, given)

    def responses(r):
        bwd.ready(1 + r)
        part = slice(r * count, (r + 1) * count)
        for h in range(heads):
            later = st[1, 1 + r, h].astype(BF16)
            fade = power(h, count - 1.0 - place_p)[:count]
            rdk[r, h] = (dk_r[h, part, :] + fade * dot_nt(rv[r, h], later)).astype(BF16)
            rdv[r, h] = (dv_r[h, part, :] + fade * dot_nn(rk[r, h], later)).astype(BF16)

    bwd.finish(1)
    responses(0)
    bwd.finish(2)
    bwd.finish(0)
    responses(1)
    bwd.ready(0)
    with jax.named_scope("end"):
        for h in range(heads):
            later = st[1, 0, h].astype(BF16)
            fade = power(h, tokens - 1.0 - place_p)
            pdk[h] = (dk_p[h] + fade * dot_nt(pv[h], later)).astype(BF16)
            pdv[h] = (dv_p[h] + fade * dot_nn(pk[h], later)).astype(BF16)
        ny, nx = grid[1], grid[0]
        sent = (
            (pair, c_s), (csend.at[:, :, pl.ds(0, ny - 1)], a1_s), (tx.at[:, :, pl.ds(0, nx - 1)], x_s),
            (psend.at[:, :, pl.ds(0, ny - 1)], a2_s), (fsend, f_s), (stat.at[:, pl.ds(0, nz - 1)], z_s),
        )
        for part, sem in sent:
            fwd.copy(part, part, sem, sem, ahead.partner()).wait_send()


def hand_over(*refs):
    copies = [pltpu.make_async_copy(src, dst, refs[16].at[i]) for i, (src, dst) in enumerate(zip(refs[:8], refs[8:16]))]
    for copy in copies:
        copy.start()
    for copy in copies:
        copy.wait()


def shards(grid, nz, prompt_q, prompt_k, prompt_v, resp_q, resp_k, resp_v, decay_rate, norm_gain, prompt_cot, resp_cot):
    nx, ny, _ = grid
    tokens, heads, width = prompt_q.shape
    count = resp_q.shape[1]
    half, rows = width // 2, width // 2 // ny
    prompt = [jnp.transpose(a, (1, 0, 2)) for a in (prompt_q, prompt_k, prompt_v, prompt_cot)]
    resp = [jnp.transpose(a, (0, 2, 1, 3)) for a in (resp_q, resp_k, resp_v, resp_cot)]
    flat = pltpu.VMEM((heads, tokens, width), BF16)
    duo = pltpu.VMEM((2, heads, count, width), BF16)
    vmem, hbm = pl.BlockSpec(memory_space=pltpu.VMEM), pl.BlockSpec(memory_space=pltpu.HBM)
    block = (heads, tokens, width)
    scratch = [pltpu.SMEM((heads,), F32), pltpu.VMEM((heads, width), F32)]
    scratch += [pltpu.VMEM(block, BF16)] * 4 + [pltpu.VMEM((2, heads, count, width), BF16)] * 4
    scratch += [
        pltpu.VMEM((2, 3, heads, width, width), F32),
        pltpu.VMEM((2, 3, heads, half, width), F32),
        pltpu.VMEM((2, 3, ny, heads, rows, width), F32),
        pltpu.VMEM((2, 3, ny, heads, rows, width), F32),
        pltpu.VMEM((2, 3, nx, heads, rows, width), F32),
        pltpu.VMEM((2, 3, ny, heads, rows, width), F32),
        pltpu.VMEM((2, 3, ny, heads, rows, width), F32),
        pltpu.VMEM((2, 3, heads, half, width), F32),
        pltpu.VMEM((2, 3, heads, width, width), F32),
        pltpu.VMEM((3, nz, 8, width), F32),
        pltpu.VMEM(block, BF16),
        pltpu.VMEM(block, BF16),
        pltpu.VMEM(block, F32),
        pltpu.VMEM(block, F32),
        pltpu.VMEM(block, BF16),
        pltpu.VMEM(block, BF16),
        pltpu.VMEM(block, F32),
        pltpu.VMEM(block, F32),
        pltpu.VMEM(block, F32),
        pltpu.VMEM(block, F32),
    ]
    dma = pltpu.SemaphoreType.DMA
    scratch += [dma((10,))] + [dma, dma((2, 3))] * 5 + [dma, dma((3,))]
    scratch += [pltpu.SemaphoreType.REGULAR((max(1, len(reaching(nz))), 2))]
    out = pl.pallas_call(
        functools.partial(kernel, grid, nz),
        out_shape=(flat, duo, flat, flat, flat, duo, duo, duo),
        in_specs=[hbm] * 10,
        out_specs=(vmem,) * 8,
        scratch_shapes=scratch,
        compiler_params=pltpu.CompilerParams(collective_id=0, has_side_effects=True, vmem_limit_bytes=40 << 20),
    )(*(pltpu.with_memory_space_constraint(a, pltpu.HBM) for a in (decay_rate, norm_gain, *prompt, *resp)))
    out = pl.pallas_call(
        hand_over,
        out_shape=tuple(jax.ShapeDtypeStruct(a.shape, a.dtype) for a in out),
        in_specs=[vmem] * 8,
        out_specs=(hbm,) * 8,
        scratch_shapes=[dma((8,))],
        compiler_params=pltpu.CompilerParams(vmem_limit_bytes=8 << 20),
    )(*out)
    return tuple(
        jnp.transpose(a, (1, 0, 2)) if a.ndim == 3 else jnp.transpose(a, (0, 2, 1, 3)) for a in out
    )


def solution(mesh):
    flat, duo = P("ctx", "head", None), P(None, "ctx", "head", None)
    return jax.shard_map(
        functools.partial(shards, GRID, mesh.shape["head"]),
        mesh=mesh,
        in_specs=(flat, flat, flat, duo, duo, duo, P("head"), P("head", None), flat, duo),
        out_specs=(flat, duo, flat, flat, flat, duo, duo, duo),
        check_vma=False,
    )
```

```python
import functools

import jax
import jax.numpy as jnp
from jax import lax
from jax.experimental import pallas as pl
from jax.experimental.pallas import tpu as pltpu
from jax.sharding import PartitionSpec as P

GRID = (4, 8, 2)
MESH = pl.DeviceIdType.MESH
F32 = jnp.float32
BF16 = jnp.bfloat16


def dot(left, right, dims):
    return lax.dot_general(left, right, (dims, ((), ())), preferred_element_type=F32)


def dot_nn(left, right):
    return dot(left, right, ((1,), (0,)))


def dot_nt(left, right):
    return dot(left, right, ((1,), (1,)))


def dot_tn(left, right):
    return dot(left, right, ((0,), (0,)))


class Place:
    def __init__(self, grid, reverse):
        self.nx, self.ny, _ = grid
        self.reverse = reverse
        ctx = lax.axis_index("ctx")
        self.head = lax.axis_index("head")
        self.core = lax.rem(ctx, 2)
        self.phys_y = lax.rem(ctx // 2, self.ny)
        self.phys_x = ctx // (2 * self.ny)
        self.y = self.ny - 1 - self.phys_y if reverse else self.phys_y
        self.x = self.nx - 1 - self.phys_x if reverse else self.phys_x
        self.order = 1 - self.core if reverse else self.core

    def device(self, x, y, core):
        return ((x * self.ny + y) * 2 + core, self.head)

    def partner(self):
        return self.device(self.phys_x, self.phys_y, 1 - self.core)

    def along_y(self, y):
        return self.device(self.phys_x, self.ny - 1 - y if self.reverse else y, self.core)

    def along_x(self, x):
        return self.device(self.nx - 1 - x if self.reverse else x, self.phys_y, self.core)


class Scan:
    def __init__(self, way, place, rate, lengths, refs):
        self.way, self.place, self.rate, self.lengths = way, place, rate, lengths
        (self.loc, self.pair, self.csend, self.a1, self.tx, self.psend, self.a2, self.fsend, self.st) = refs[:9]
        (self.c_s, self.c_r, self.a1_s, self.a1_r, self.x_s, self.x_r, self.a2_s, self.a2_r, self.f_s, self.f_r) = refs[9:]
        self.heads = self.loc.shape[2]
        self.rows = self.csend.shape[4]
        self.half = self.fsend.shape[3]
        self.name = ("fwd", "bwd")[way]

    def decay(self, h, tokens):
        return jnp.exp(jnp.full((1, 128), -self.rate[h], F32) * tokens)

    def copy(self, src, dst, send, recv, device):
        return pltpu.make_async_remote_copy(
            src_ref=src, dst_ref=dst, send_sem=send, recv_sem=recv, device_id=device, device_id_type=MESH
        )

    def half_of(self, core):
        return pl.ds(pl.multiple_of(core * self.half, self.half), self.half)

    def pair_copy(self, s):
        w, p = self.way, self.place
        src = self.loc.at[w, s, :, self.half_of(1 - p.core), :]
        return self.copy(src, self.pair.at[w, s], self.c_s, self.c_r.at[w, s], p.partner())

    def start_pair(self, s):
        self.pair_copy(s).start()

    def first_second(self, s, h):
        own = self.loc[self.way, s, h, self.half_of(self.place.core), :]
        other = self.pair[self.way, s, h]
        leads = self.place.order == 0
        return jnp.where(leads, own, other), jnp.where(leads, other, own)

    def send_along_y(self, src, dst, send, recv, s):
        w, p = self.way, self.place
        for k in far_first(p.ny):
            to = lax.rem(p.y + k, p.ny)
            self.copy(src.at[w, s, to], dst.at[w, s, p.y], send, recv.at[w, s], p.along_y(to)).start()

    def wait_all(self, buf, sem, s):
        others = buf.at[self.way, s, pl.ds(0, buf.shape[2] - 1)]
        self.copy(others, others, sem.at[self.way, s], sem.at[self.way, s], self.place.partner()).wait_recv()

    def chip(self, s):
        w, p = self.way, self.place
        with jax.named_scope(f"{self.name}_pair{s}"):
            self.pair_copy(s).wait_recv()
        for h in range(self.heads):
            first, second = self.first_second(s, h)
            both = self.decay(h, float(self.lengths[s])) * first + second
            for j in range(p.ny):
                self.csend[w, s, j, h] = both[j * self.rows : (j + 1) * self.rows]
        self.a1[w, s, p.y] = self.csend[w, s, p.y]
        self.send_along_y(self.csend, self.a1, self.a1_s, self.a1_r, s)

    def column(self, s):
        w, p = self.way, self.place
        with jax.named_scope(f"{self.name}_gather{s}"):
            self.wait_all(self.a1, self.a1_r, s)
        for h in range(self.heads):
            step = self.decay(h, 2.0 * self.lengths[s])
            total = self.a1[w, s, 0, h]
            for j in range(1, p.ny):
                total = step * total + self.a1[w, s, j, h]
            self.tx[w, s, p.x, h] = total
        for k in far_first(p.nx):
            to = lax.rem(p.x + k, p.nx)
            mine = self.tx.at[w, s, p.x]
            self.copy(mine, mine, self.x_s, self.x_r.at[w, s], p.along_x(to)).start()

    def columns(self, s):
        w, p = self.way, self.place
        with jax.named_scope(f"{self.name}_x{s}"):
            self.wait_all(self.tx, self.x_r, s)
        bases, totals = [], []
        for h in range(self.heads):
            step = self.decay(h, 2.0 * self.lengths[s] * p.ny)
            run = self.tx[w, s, 0, h]
            base = jnp.zeros_like(run)
            for j in range(1, p.nx):
                base = jnp.where(p.x == j, run, base)
                run = step * run + self.tx[w, s, j, h]
            bases.append(base)
            totals.append(run)
        return bases, totals

    def spread(self, s, bases, given):
        w, p = self.way, self.place
        for h in range(self.heads):
            step = self.decay(h, 2.0 * self.lengths[s])
            entry = bases[h]
            if given is not None:
                before = (p.x * (2 * p.ny * self.lengths[s])).astype(F32)
                entry = entry + self.decay(h, before) * given[h]
            for j in range(p.ny):
                self.psend[w, s, j, h] = entry
                if j < p.ny - 1:
                    entry = step * entry + self.a1[w, s, j, h]
        self.a2[w, s, p.y] = self.psend[w, s, p.y]
        self.send_along_y(self.psend, self.a2, self.a2_s, self.a2_r, s)

    def final_copy(self, s):
        w, p = self.way, self.place
        dst = self.st.at[w, s, :, self.half_of(p.core), :]
        return self.copy(self.fsend.at[w, s], dst, self.f_s, self.f_r.at[w, s], p.partner())

    def finish(self, s):
        w, p = self.way, self.place
        with jax.named_scope(f"{self.name}_spread{s}"):
            self.wait_all(self.a2, self.a2_r, s)
        leads = p.order == 0
        for h in range(self.heads):
            entry = jnp.concatenate([self.a2[w, s, j, h] for j in range(p.ny)], axis=0)
            first, _ = self.first_second(s, h)
            after = self.decay(h, float(self.lengths[s])) * entry + first
            self.st[w, s, h, self.half_of(p.core), :] = jnp.where(leads, entry, after)
            self.fsend[w, s, h] = jnp.where(leads, after, entry)
        self.final_copy(s).start()

    def ready(self, s):
        w, p = self.way, self.place
        landed = self.st.at[w, s, :, self.half_of(1 - p.core), :]
        with jax.named_scope(f"{self.name}_last{s}"):
            self.copy(landed, landed, self.f_r.at[w, s], self.f_r.at[w, s], p.partner()).wait_recv()


def far_first(n):
    return sorted(range(1, n), key=lambda k: -min(k, n - k))


def reaching(n):
    strides, reach = [], 1
    while reach < n // 2:
        strides.append(min(reach, n // 2 - reach))
        reach += strides[-1]
    return strides


def column_of(row):
    return jnp.broadcast_to(row, (128, 128)).T


def kernel(
    grid, nz, *refs
):
    places = refs[:10]
    py, ry, pdq, pdk, pdv, rdq, rdk, rdv = refs[10:18]
    held = refs[18:28]
    rate, gain, pq, pk, pv, pc, rq, rk, rv, rc = held
    loc, pair, csend, a1, tx, psend, a2, fsend, st, stat, pmix, rmix, pout, rout, pgrad, rgrad, dk_p, dv_p, dk_r, dv_r, pfade, rfade = refs[28:50]
    in_s, c_s, c_r, a1_s, a1_r, x_s, x_r, a2_s, a2_r, f_s, f_r, z_s, z_r, told = refs[50:]
    def arrive(*wanted):
        for ref in wanted:
            loads[id(ref)].wait()

    heads, tokens, width = pq.shape
    count = rq.shape[2]
    features = float(heads * nz * width)
    ahead, back = Place(grid, False), Place(grid, True)
    ctx, z = lax.axis_index("ctx"), ahead.head

    barrier = pltpu.get_barrier_semaphore()
    peers = [ahead.along_y(lax.rem(ahead.y + k, grid[1])) for k in far_first(grid[1])]
    peers += [ahead.along_x(lax.rem(ahead.x + k, grid[0])) for k in range(1, grid[0])]
    peers += [ahead.partner(), (ctx, lax.rem(z + 1, nz)), (ctx, lax.rem(z + nz - 1, nz))]
    for peer in peers:
        pl.semaphore_signal(barrier, inc=1, device_id=peer, device_id_type=MESH)

    loads = {id(dst): pltpu.make_async_copy(src, dst, in_s.at[i]) for i, (src, dst) in enumerate(zip(places, held))}
    for ref in (rate, pk, pv, rk, rv, gain, pq, rq, pc, rc):
        loads[id(ref)].start()

    refs = (loc, pair, csend, a1, tx, psend, a2, fsend, st, c_s, c_r, a1_s, a1_r, x_s, x_r, a2_s, a2_r, f_s, f_r)
    lengths = (tokens, count, count)
    fwd = Scan(0, ahead, rate, lengths, refs)
    bwd = Scan(1, back, rate, lengths, refs)

    row = lax.broadcasted_iota(jnp.int32, (128, 128), 0)
    col = lax.broadcasted_iota(jnp.int32, (128, 128), 1)
    lag = (row - col).astype(F32)
    causal = row >= col
    apart = (row // count) != (col // count)
    place_p = row.astype(F32)
    place_r = lax.rem(row, count).astype(F32)

    def power(h, steps):
        return jnp.exp(jnp.full((128, 128), -rate[h], F32) * steps)

    def pairs(ref, h):
        return jnp.concatenate([ref[0, h], ref[1, h]], axis=0)

    def masks(h):
        mask = jnp.where(causal, power(h, jnp.maximum(lag, 0.0)), 0.0)
        return mask, jnp.where(apart, 0.0, mask)

    strides = reaching(nz)

    def tell(i):
        for side, stride in enumerate((strides[i], nz - strides[i])):
            to = (ctx, lax.rem(z + stride, nz))
            pl.semaphore_signal(told.at[i, side], inc=1, device_id=to, device_id_type=MESH)

    def hear(i):
        with jax.named_scope(f"hear{i}"):
            for side in range(2):
                pl.semaphore_wait(told.at[i, side], 1)
        if i + 1 < len(strides):
            tell(i + 1)

    def fwd_states(s):
        for h in range(heads):
            if s == 0:
                keys = (pk[h].astype(F32) * power(h, tokens - 1.0 - place_p)).astype(BF16)
                loc[0, 0, h] = dot_tn(keys, pv[h])
            else:
                keys = (rk[s - 1, h].astype(F32) * power(h, count - 1.0 - place_p)[:count]).astype(BF16)
                loc[0, s, h] = dot_tn(keys, rv[s - 1, h])

    with jax.named_scope("local_p"):
        arrive(rate, pk, pv)
        fwd_states(0)
    with jax.named_scope("entry"):
        pl.semaphore_wait(barrier, len(peers))
    fwd.start_pair(0)
    if strides:
        tell(0)
    with jax.named_scope("local_r"):
        arrive(rk, rv)
        fwd_states(1)
        fwd.start_pair(1)
        fwd_states(2)
        fwd.start_pair(2)
    for s in range(3):
        fwd.chip(s)
    if strides:
        hear(0)

    with jax.named_scope("intra"):
        arrive(pq, rq)
        for h in range(heads):
            mask_p, mask_r = masks(h)
            pmix[h] = (dot_nt(pq[h], pk[h]) * mask_p).astype(BF16)
            rmix[h] = (dot_nt(pairs(rq, h), pairs(rk, h)) * mask_r).astype(BF16)
            pout[h] = dot_nn(pmix[h], pv[h])
            rout[h] = dot_nn(rmix[h], pairs(rv, h))
            pfade[h] = (pq[h].astype(F32) * power(h, place_p + 1.0)).astype(BF16)
            rfade[h] = (pairs(rq, h).astype(F32) * power(h, place_r + 1.0)).astype(BF16)

    arrive(gain, pc, rc)
    if len(strides) > 1:
        hear(1)
    fwd.column(0)
    for i in range(2, len(strides)):
        hear(i)
    fwd.column(1)
    bases, final = fwd.columns(0)
    fwd.spread(0, bases, None)
    fwd.column(2)
    for s in (1, 2):
        bases, _ = fwd.columns(s)
        fwd.spread(s, bases, final)

    def outputs(s):
        fwd.ready(s)
        rows = tokens if s == 0 else count
        part = slice(0, rows) if s == 0 else slice((s - 1) * count, s * count)
        squares, inner = jnp.zeros((rows, 128), F32), jnp.zeros((rows, 128), F32)
        for h in range(heads):
            buf = pout if s == 0 else rout
            queries, cot = (pq[h], pc[h]) if s == 0 else (rq[s - 1, h], rc[s - 1, h])
            across = dot_nn(queries, st[0, s, h].astype(BF16))
            out = buf[h, part, :] + power(h, place_p + 1.0)[:rows] * across
            buf[h, part, :] = out
            squares += out * out
            inner += gain[h : h + 1] * cot.astype(F32) * out
        both = [squares, inner] if s == 0 else [jnp.concatenate([squares, inner], axis=0)]
        lines = [jnp.sum(a.T, axis=0, keepdims=True) for a in both]
        stat[s, z] = jnp.concatenate(lines + [jnp.zeros((8 - len(lines), 128), F32)], axis=0)
        for k in far_first(nz):
            to = (ctx, lax.rem(z + k, nz))
            fwd.copy(stat.at[s, z], stat.at[s, z], z_s, z_r.at[s], to).start()

    def norms(s):
        with jax.named_scope(f"norm{s}"):
            others = stat.at[s, pl.ds(0, nz - 1)]
            fwd.copy(others, others, z_r.at[s], z_r.at[s], ahead.partner()).wait_recv()
        total = stat[s, 0]
        for k in range(1, nz):
            total = total + stat[s, k]
        if s == 0:
            inv = lax.rsqrt(total[0:1] / features + 1e-05)
            return column_of(inv), column_of(total[1:2] * inv * inv * inv / features)
        both = column_of(total[0:1])
        inv = lax.rsqrt(both[:count] / features + 1e-05)
        return inv, both[count:] * inv * inv * inv / features

    def gradients(s):
        inv, coef = norms(s)
        rows = tokens if s == 0 else count
        part = slice(0, rows) if s == 0 else slice((s - 1) * count, s * count)
        for h in range(heads):
            out = (pout if s == 0 else rout)[h, part, :]
            cot = pc[h] if s == 0 else rc[s - 1, h]
            grad = (gain[h : h + 1] * cot.astype(F32) * inv - out * coef).astype(BF16)
            if s == 0:
                pgrad[h] = grad
            else:
                rgrad[h, part, :] = grad
            loc[1, s, h] = dot_tn(pfade[h] if s == 0 else rfade[h, part, :], grad)
        bwd.start_pair(s)
        return inv

    def normed(s, inv):
        for h in range(heads):
            if s == 0:
                py[h] = (gain[h : h + 1] * pout[h] * inv).astype(BF16)
            else:
                ry[s - 1, h] = (gain[h : h + 1] * rout[h, (s - 1) * count : s * count, :] * inv).astype(BF16)

    for s in range(3):
        fwd.finish(s)
        outputs(s)
    scales = []
    for s in range(3):
        scales.append(gradients(s))
        bwd.chip(s)

    with jax.named_scope("inner"):
        for s, inv in enumerate(scales):
            normed(s, inv)
        for h in range(heads):
            mask_p, mask_r = masks(h)
            grad = pgrad[h]
            dmix = (dot_nt(grad, pv[h]) * mask_p).astype(BF16)
            across = dot_nt(grad, st[0, 0, h].astype(BF16))
            pdq[h] = (dot_nn(dmix, pk[h]) + power(h, place_p + 1.0) * across).astype(BF16)
            dk_p[h] = dot_tn(dmix, pq[h])
            dv_p[h] = dot_tn(pmix[h], grad)
            grad = rgrad[h]
            dmix = (dot_nt(grad, pairs(rv, h)) * mask_r).astype(BF16)
            across = [dot_nt(grad[r * count : (r + 1) * count], st[0, 1 + r, h].astype(BF16)) for r in range(2)]
            queries = dot_nn(dmix, pairs(rk, h)) + power(h, place_r + 1.0) * jnp.concatenate(across, axis=0)
            dk_r[h] = dot_tn(dmix, pairs(rq, h))
            dv_r[h] = dot_tn(rmix[h], grad)
            for r in range(2):
                rdq[r, h] = queries[r * count : (r + 1) * count].astype(BF16)

    bwd.column(0)
    bwd.column(1)
    bwd.column(2)
    bases_0, totals_0 = bwd.columns(1)
    bwd.spread(1, bases_0, None)
    bases_1, totals_1 = bwd.columns(2)
    bases, _ = bwd.columns(0)
    bwd.spread(0, bases, [a + b for a, b in zip(totals_0, totals_1)])
    bwd.spread(2, bases_1, None)

    def responses(r):
        bwd.ready(1 + r)
        part = slice(r * count, (r + 1) * count)
        for h in range(heads):
            later = st[1, 1 + r, h].astype(BF16)
            fade = power(h, count - 1.0 - place_p)[:count]
            rdk[r, h] = (dk_r[h, part, :] + fade * dot_nt(rv[r, h], later)).astype(BF16)
            rdv[r, h] = (dv_r[h, part, :] + fade * dot_nn(rk[r, h], later)).astype(BF16)

    ny, nx = grid[1], grid[0]

    def sent(part, sem):
        fwd.copy(part, part, sem, sem, ahead.partner()).wait_send()

    sent(pair, c_s)
    sent(csend.at[:, :, pl.ds(0, ny - 1)], a1_s)
    sent(tx.at[:, :, pl.ds(0, nx - 1)], x_s)
    sent(stat.at[:, pl.ds(0, nz - 1)], z_s)
    bwd.finish(1)
    responses(0)
    bwd.finish(0)
    bwd.finish(2)
    bwd.ready(0)
    with jax.named_scope("end"):
        for h in range(heads):
            later = st[1, 0, h].astype(BF16)
            fade = power(h, tokens - 1.0 - place_p)
            pdk[h] = (dk_p[h] + fade * dot_nt(pv[h], later)).astype(BF16)
            pdv[h] = (dv_p[h] + fade * dot_nn(pk[h], later)).astype(BF16)
    responses(1)
    sent(psend.at[:, :, pl.ds(0, ny - 1)], a2_s)
    sent(fsend, f_s)


def hand_over(*refs):
    copies = [pltpu.make_async_copy(src, dst, refs[16].at[i]) for i, (src, dst) in enumerate(zip(refs[:8], refs[8:16]))]
    for copy in copies:
        copy.start()
    for copy in copies:
        copy.wait()


def shards(grid, nz, prompt_q, prompt_k, prompt_v, resp_q, resp_k, resp_v, decay_rate, norm_gain, prompt_cot, resp_cot):
    nx, ny, _ = grid
    tokens, heads, width = prompt_q.shape
    count = resp_q.shape[1]
    half, rows = width // 2, width // 2 // ny
    prompt = [jnp.transpose(a, (1, 0, 2)) for a in (prompt_q, prompt_k, prompt_v, prompt_cot)]
    resp = [jnp.transpose(a, (0, 2, 1, 3)) for a in (resp_q, resp_k, resp_v, resp_cot)]
    flat = pltpu.VMEM((heads, tokens, width), BF16)
    duo = pltpu.VMEM((2, heads, count, width), BF16)
    vmem, hbm = pl.BlockSpec(memory_space=pltpu.VMEM), pl.BlockSpec(memory_space=pltpu.HBM)
    block = (heads, tokens, width)
    scratch = [pltpu.SMEM((heads,), F32), pltpu.VMEM((heads, width), F32)]
    scratch += [pltpu.VMEM(block, BF16)] * 4 + [pltpu.VMEM((2, heads, count, width), BF16)] * 4
    scratch += [
        pltpu.VMEM((2, 3, heads, width, width), F32),
        pltpu.VMEM((2, 3, heads, half, width), F32),
        pltpu.VMEM((2, 3, ny, heads, rows, width), F32),
        pltpu.VMEM((2, 3, ny, heads, rows, width), F32),
        pltpu.VMEM((2, 3, nx, heads, rows, width), F32),
        pltpu.VMEM((2, 3, ny, heads, rows, width), F32),
        pltpu.VMEM((2, 3, ny, heads, rows, width), F32),
        pltpu.VMEM((2, 3, heads, half, width), F32),
        pltpu.VMEM((2, 3, heads, width, width), F32),
        pltpu.VMEM((3, nz, 8, width), F32),
        pltpu.VMEM(block, BF16),
        pltpu.VMEM(block, BF16),
        pltpu.VMEM(block, F32),
        pltpu.VMEM(block, F32),
        pltpu.VMEM(block, BF16),
        pltpu.VMEM(block, BF16),
        pltpu.VMEM(block, F32),
        pltpu.VMEM(block, F32),
        pltpu.VMEM(block, F32),
        pltpu.VMEM(block, F32),
    ]
    scratch += [pltpu.VMEM(block, BF16)] * 2
    dma = pltpu.SemaphoreType.DMA
    scratch += [dma((10,))] + [dma, dma((2, 3))] * 5 + [dma, dma((3,))]
    scratch += [pltpu.SemaphoreType.REGULAR((max(1, len(reaching(nz))), 2))]
    out = pl.pallas_call(
        functools.partial(kernel, grid, nz),
        out_shape=(flat, duo, flat, flat, flat, duo, duo, duo),
        in_specs=[hbm] * 10,
        out_specs=(vmem,) * 8,
        scratch_shapes=scratch,
        compiler_params=pltpu.CompilerParams(collective_id=0, has_side_effects=True, vmem_limit_bytes=40 << 20),
    )(*(pltpu.with_memory_space_constraint(a, pltpu.HBM) for a in (decay_rate, norm_gain, *prompt, *resp)))
    out = pl.pallas_call(
        hand_over,
        out_shape=tuple(jax.ShapeDtypeStruct(a.shape, a.dtype) for a in out),
        in_specs=[vmem] * 8,
        out_specs=(hbm,) * 8,
        scratch_shapes=[dma((8,))],
        compiler_params=pltpu.CompilerParams(vmem_limit_bytes=8 << 20),
    )(*out)
    return tuple(
        jnp.transpose(a, (1, 0, 2)) if a.ndim == 3 else jnp.transpose(a, (0, 2, 1, 3)) for a in out
    )


def solution(mesh):
    flat, duo = P("ctx", "head", None), P(None, "ctx", "head", None)
    return jax.shard_map(
        functools.partial(shards, GRID, mesh.shape["head"]),
        mesh=mesh,
        in_specs=(flat, flat, flat, duo, duo, duo, P("head"), P("head", None), flat, duo),
        out_specs=(flat, duo, flat, flat, flat, duo, duo, duo),
        check_vma=False,
    )
```

```python
import functools

import jax
import jax.numpy as jnp
from jax import lax
from jax.experimental import pallas as pl
from jax.experimental.pallas import tpu as pltpu
from jax.sharding import PartitionSpec as P

GRID = (4, 8, 2)
MESH = pl.DeviceIdType.MESH
F32 = jnp.float32
BF16 = jnp.bfloat16


def dot(left, right, dims):
    return lax.dot_general(left, right, (dims, ((), ())), preferred_element_type=F32)


def dot_nn(left, right):
    return dot(left, right, ((1,), (0,)))


def dot_nt(left, right):
    return dot(left, right, ((1,), (1,)))


def dot_tn(left, right):
    return dot(left, right, ((0,), (0,)))


class Place:
    def __init__(self, grid, reverse):
        self.nx, self.ny, _ = grid
        self.reverse = reverse
        ctx = lax.axis_index("ctx")
        self.head = lax.axis_index("head")
        self.core = lax.rem(ctx, 2)
        self.phys_y = lax.rem(ctx // 2, self.ny)
        self.phys_x = ctx // (2 * self.ny)
        self.y = self.ny - 1 - self.phys_y if reverse else self.phys_y
        self.x = self.nx - 1 - self.phys_x if reverse else self.phys_x
        self.order = 1 - self.core if reverse else self.core

    def device(self, x, y, core):
        return ((x * self.ny + y) * 2 + core, self.head)

    def partner(self):
        return self.device(self.phys_x, self.phys_y, 1 - self.core)

    def along_y(self, y):
        return self.device(self.phys_x, self.ny - 1 - y if self.reverse else y, self.core)

    def along_x(self, x):
        return self.device(self.nx - 1 - x if self.reverse else x, self.phys_y, self.core)


class Scan:
    def __init__(self, way, place, rate, lengths, refs):
        self.way, self.place, self.rate, self.lengths = way, place, rate, lengths
        (self.loc, self.pair, self.csend, self.a1, self.tx, self.psend, self.a2, self.fsend, self.st) = refs[:9]
        (self.c_s, self.c_r, self.a1_s, self.a1_r, self.x_s, self.x_r, self.a2_s, self.a2_r, self.f_s, self.f_r) = refs[9:]
        self.heads = self.loc.shape[2]
        self.rows = self.csend.shape[4]
        self.half = self.fsend.shape[3]
        self.name = ("fwd", "bwd")[way]

    def decay(self, h, tokens):
        return jnp.exp(jnp.full((1, 128), -self.rate[h], F32) * tokens)

    def copy(self, src, dst, send, recv, device):
        return pltpu.make_async_remote_copy(
            src_ref=src, dst_ref=dst, send_sem=send, recv_sem=recv, device_id=device, device_id_type=MESH
        )

    def half_of(self, core):
        return pl.ds(pl.multiple_of(core * self.half, self.half), self.half)

    def pair_copy(self, s):
        w, p = self.way, self.place
        src = self.loc.at[w, s, :, self.half_of(1 - p.core), :]
        return self.copy(src, self.pair.at[w, s], self.c_s, self.c_r.at[w, s], p.partner())

    def start_pair(self, s):
        self.pair_copy(s).start()

    def first_second(self, s, h):
        own = self.loc[self.way, s, h, self.half_of(self.place.core), :]
        other = self.pair[self.way, s, h]
        leads = self.place.order == 0
        return jnp.where(leads, own, other), jnp.where(leads, other, own)

    def send_along_y(self, src, dst, send, recv, s):
        w, p = self.way, self.place
        for k in far_first(p.ny):
            to = lax.rem(p.y + k, p.ny)
            self.copy(src.at[w, s, to], dst.at[w, s, p.y], send, recv.at[w, s], p.along_y(to)).start()

    def wait_all(self, buf, sem, s):
        others = buf.at[self.way, s, pl.ds(0, buf.shape[2] - 1)]
        self.copy(others, others, sem.at[self.way, s], sem.at[self.way, s], self.place.partner()).wait_recv()

    def chip(self, s):
        w, p = self.way, self.place
        with jax.named_scope(f"{self.name}_pair{s}"):
            self.pair_copy(s).wait_recv()
        for h in range(self.heads):
            first, second = self.first_second(s, h)
            both = self.decay(h, float(self.lengths[s])) * first + second
            for j in range(p.ny):
                self.csend[w, s, j, h] = both[j * self.rows : (j + 1) * self.rows]
        self.a1[w, s, p.y] = self.csend[w, s, p.y]
        self.send_along_y(self.csend, self.a1, self.a1_s, self.a1_r, s)

    def column(self, s):
        w, p = self.way, self.place
        with jax.named_scope(f"{self.name}_gather{s}"):
            self.wait_all(self.a1, self.a1_r, s)
        for h in range(self.heads):
            step = self.decay(h, 2.0 * self.lengths[s])
            total = self.a1[w, s, 0, h]
            for j in range(1, p.ny):
                total = step * total + self.a1[w, s, j, h]
            self.tx[w, s, p.x, h] = total
        for k in far_first(p.nx):
            to = lax.rem(p.x + k, p.nx)
            mine = self.tx.at[w, s, p.x]
            self.copy(mine, mine, self.x_s, self.x_r.at[w, s], p.along_x(to)).start()

    def columns(self, s):
        w, p = self.way, self.place
        with jax.named_scope(f"{self.name}_x{s}"):
            self.wait_all(self.tx, self.x_r, s)
        bases, totals = [], []
        for h in range(self.heads):
            step = self.decay(h, 2.0 * self.lengths[s] * p.ny)
            run = self.tx[w, s, 0, h]
            base = jnp.zeros_like(run)
            for j in range(1, p.nx):
                base = jnp.where(p.x == j, run, base)
                run = step * run + self.tx[w, s, j, h]
            bases.append(base)
            totals.append(run)
        return bases, totals

    def spread(self, s, bases, given):
        w, p = self.way, self.place
        for h in range(self.heads):
            step = self.decay(h, 2.0 * self.lengths[s])
            entry = bases[h]
            if given is not None:
                before = (p.x * (2 * p.ny * self.lengths[s])).astype(F32)
                entry = entry + self.decay(h, before) * given[h]
            for j in range(p.ny):
                self.psend[w, s, j, h] = entry
                if j < p.ny - 1:
                    entry = step * entry + self.a1[w, s, j, h]
        self.a2[w, s, p.y] = self.psend[w, s, p.y]
        self.send_along_y(self.psend, self.a2, self.a2_s, self.a2_r, s)

    def final_copy(self, s):
        w, p = self.way, self.place
        dst = self.st.at[w, s, :, self.half_of(p.core), :]
        return self.copy(self.fsend.at[w, s], dst, self.f_s, self.f_r.at[w, s], p.partner())

    def finish(self, s):
        w, p = self.way, self.place
        with jax.named_scope(f"{self.name}_spread{s}"):
            self.wait_all(self.a2, self.a2_r, s)
        leads = p.order == 0
        for h in range(self.heads):
            entry = jnp.concatenate([self.a2[w, s, j, h] for j in range(p.ny)], axis=0)
            first, _ = self.first_second(s, h)
            after = self.decay(h, float(self.lengths[s])) * entry + first
            self.st[w, s, h, self.half_of(p.core), :] = jnp.where(leads, entry, after)
            self.fsend[w, s, h] = jnp.where(leads, after, entry)
        self.final_copy(s).start()

    def ready(self, s):
        w, p = self.way, self.place
        landed = self.st.at[w, s, :, self.half_of(1 - p.core), :]
        with jax.named_scope(f"{self.name}_last{s}"):
            self.copy(landed, landed, self.f_r.at[w, s], self.f_r.at[w, s], p.partner()).wait_recv()


def far_first(n):
    return sorted(range(1, n), key=lambda k: -min(k, n - k))


def reaching(n):
    strides, reach = [], 1
    while reach < n // 2:
        strides.append(min(reach, n // 2 - reach))
        reach += strides[-1]
    return strides


def column_of(row):
    return jnp.broadcast_to(row, (128, 128)).T


def kernel(
    grid, nz, *refs
):
    places = refs[:10]
    py, ry, pdq, pdk, pdv, rdq, rdk, rdv = refs[10:18]
    held = refs[18:28]
    rate, gain, pq, pk, pv, pc, rq, rk, rv, rc = held
    loc, pair, csend, a1, tx, psend, a2, fsend, st, stat, pmix, rmix, pout, rout, pgrad, rgrad, dk_p, dv_p, dk_r, dv_r, pfade, rfade, pstep, rstep, pcot, rcot = refs[28:54]
    in_s, c_s, c_r, a1_s, a1_r, x_s, x_r, a2_s, a2_r, f_s, f_r, z_s, z_r, told = refs[54:]
    def arrive(*wanted):
        for ref in wanted:
            loads[id(ref)].wait()

    heads, tokens, width = pq.shape
    count = rq.shape[2]
    features = float(heads * nz * width)
    ahead, back = Place(grid, False), Place(grid, True)
    ctx, z = lax.axis_index("ctx"), ahead.head

    barrier = pltpu.get_barrier_semaphore()
    peers = [ahead.along_y(lax.rem(ahead.y + k, grid[1])) for k in far_first(grid[1])]
    peers += [ahead.along_x(lax.rem(ahead.x + k, grid[0])) for k in range(1, grid[0])]
    peers += [ahead.partner(), (ctx, lax.rem(z + 1, nz)), (ctx, lax.rem(z + nz - 1, nz))]
    for peer in peers:
        pl.semaphore_signal(barrier, inc=1, device_id=peer, device_id_type=MESH)

    loads = {id(dst): pltpu.make_async_copy(src, dst, in_s.at[i]) for i, (src, dst) in enumerate(zip(places, held))}
    for ref in (rate, pk, pv, rk, rv, gain, pq, rq, pc, rc):
        loads[id(ref)].start()

    refs = (loc, pair, csend, a1, tx, psend, a2, fsend, st, c_s, c_r, a1_s, a1_r, x_s, x_r, a2_s, a2_r, f_s, f_r)
    lengths = (tokens, count, count)
    fwd = Scan(0, ahead, rate, lengths, refs)
    bwd = Scan(1, back, rate, lengths, refs)

    row = lax.broadcasted_iota(jnp.int32, (128, 128), 0)
    col = lax.broadcasted_iota(jnp.int32, (128, 128), 1)
    lag = (row - col).astype(F32)
    causal = row >= col
    apart = (row // count) != (col // count)
    place_p = row.astype(F32)
    place_r = lax.rem(row, count).astype(F32)

    def power(h, steps):
        return jnp.exp(jnp.full((128, 128), -rate[h], F32) * steps)

    def pairs(ref, h):
        return jnp.concatenate([ref[0, h], ref[1, h]], axis=0)

    def masks(h):
        mask = jnp.where(causal, power(h, jnp.maximum(lag, 0.0)), 0.0)
        return mask, jnp.where(apart, 0.0, mask)

    strides = reaching(nz)

    def tell(i):
        for side, stride in enumerate((strides[i], nz - strides[i])):
            to = (ctx, lax.rem(z + stride, nz))
            pl.semaphore_signal(told.at[i, side], inc=1, device_id=to, device_id_type=MESH)

    def hear(i):
        with jax.named_scope(f"hear{i}"):
            for side in range(2):
                pl.semaphore_wait(told.at[i, side], 1)
        if i + 1 < len(strides):
            tell(i + 1)

    def fwd_states(s):
        for h in range(heads):
            if s == 0:
                keys = (pk[h].astype(F32) * power(h, tokens - 1.0 - place_p)).astype(BF16)
                loc[0, 0, h] = dot_tn(keys, pv[h])
            else:
                keys = (rk[s - 1, h].astype(F32) * power(h, count - 1.0 - place_p)[:count]).astype(BF16)
                loc[0, s, h] = dot_tn(keys, rv[s - 1, h])

    with jax.named_scope("local_p"):
        arrive(rate, pk, pv)
        fwd_states(0)
    with jax.named_scope("entry"):
        pl.semaphore_wait(barrier, len(peers))
    fwd.start_pair(0)
    if strides:
        tell(0)
    with jax.named_scope("local_r"):
        arrive(rk, rv)
        fwd_states(1)
        fwd.start_pair(1)
        fwd_states(2)
        fwd.start_pair(2)
    for s in range(3):
        fwd.chip(s)
    if strides:
        hear(0)

    with jax.named_scope("intra"):
        arrive(pq, rq, gain, pc, rc)
        for h in range(heads):
            mask_p, mask_r = masks(h)
            pmix[h] = (dot_nt(pq[h], pk[h]) * mask_p).astype(BF16)
            rmix[h] = (dot_nt(pairs(rq, h), pairs(rk, h)) * mask_r).astype(BF16)
            pout[h] = dot_nn(pmix[h], pv[h])
            rout[h] = dot_nn(rmix[h], pairs(rv, h))
            pstep[h] = power(h, place_p + 1.0)
            rstep[h] = power(h, place_r + 1.0)
            pfade[h] = (pq[h].astype(F32) * pstep[h]).astype(BF16)
            rfade[h] = (pairs(rq, h).astype(F32) * rstep[h]).astype(BF16)
            pcot[h] = gain[h : h + 1] * pc[h].astype(F32)
            rcot[h] = gain[h : h + 1] * pairs(rc, h).astype(F32)

    if len(strides) > 1:
        hear(1)
    fwd.column(0)
    for i in range(2, len(strides)):
        hear(i)
    fwd.column(1)
    bases, final = fwd.columns(0)
    fwd.spread(0, bases, None)
    fwd.column(2)
    for s in (1, 2):
        bases, _ = fwd.columns(s)
        fwd.spread(s, bases, final)

    def outputs(s):
        fwd.ready(s)
        rows = tokens if s == 0 else count
        part = slice(0, rows) if s == 0 else slice((s - 1) * count, s * count)
        squares, inner = jnp.zeros((rows, 128), F32), jnp.zeros((rows, 128), F32)
        for h in range(heads):
            buf = pout if s == 0 else rout
            queries, cot = (pq[h], pcot[h]) if s == 0 else (rq[s - 1, h], rcot[h, part, :])
            step = pstep[h] if s == 0 else rstep[h, part, :]
            across = dot_nn(queries, st[0, s, h].astype(BF16))
            out = buf[h, part, :] + step * across
            buf[h, part, :] = out
            squares += out * out
            inner += cot * out
        both = [squares, inner] if s == 0 else [jnp.concatenate([squares, inner], axis=0)]
        lines = [jnp.sum(a.T, axis=0, keepdims=True) for a in both]
        stat[s, z] = jnp.concatenate(lines + [jnp.zeros((8 - len(lines), 128), F32)], axis=0)
        for k in far_first(nz):
            to = (ctx, lax.rem(z + k, nz))
            fwd.copy(stat.at[s, z], stat.at[s, z], z_s, z_r.at[s], to).start()

    def norms(s):
        with jax.named_scope(f"norm{s}"):
            others = stat.at[s, pl.ds(0, nz - 1)]
            fwd.copy(others, others, z_r.at[s], z_r.at[s], ahead.partner()).wait_recv()
        total = stat[s, 0]
        for k in range(1, nz):
            total = total + stat[s, k]
        if s == 0:
            inv = lax.rsqrt(total[0:1] / features + 1e-05)
            return column_of(inv), column_of(total[1:2] * inv * inv * inv / features)
        both = column_of(total[0:1])
        inv = lax.rsqrt(both[:count] / features + 1e-05)
        return inv, both[count:] * inv * inv * inv / features

    def gradients(s):
        inv, coef = norms(s)
        rows = tokens if s == 0 else count
        part = slice(0, rows) if s == 0 else slice((s - 1) * count, s * count)
        for h in range(heads):
            out = (pout if s == 0 else rout)[h, part, :]
            cot = pcot[h] if s == 0 else rcot[h, part, :]
            grad = (cot * inv - out * coef).astype(BF16)
            if s == 0:
                pgrad[h] = grad
            else:
                rgrad[h, part, :] = grad
            loc[1, s, h] = dot_tn(pfade[h] if s == 0 else rfade[h, part, :], grad)
        bwd.start_pair(s)
        return inv

    def normed(s, inv):
        for h in range(heads):
            if s == 0:
                py[h] = (gain[h : h + 1] * pout[h] * inv).astype(BF16)
            else:
                ry[s - 1, h] = (gain[h : h + 1] * rout[h, (s - 1) * count : s * count, :] * inv).astype(BF16)

    for s in range(3):
        fwd.finish(s)
        outputs(s)
    scales = []
    for s in range(3):
        scales.append(gradients(s))
        bwd.chip(s)

    with jax.named_scope("inner"):
        for s, inv in enumerate(scales):
            normed(s, inv)
        for h in range(heads):
            mask_p, mask_r = masks(h)
            grad = pgrad[h]
            dmix = (dot_nt(grad, pv[h]) * mask_p).astype(BF16)
            across = dot_nt(grad, st[0, 0, h].astype(BF16))
            pdq[h] = (dot_nn(dmix, pk[h]) + pstep[h] * across).astype(BF16)
            dk_p[h] = dot_tn(dmix, pq[h])
            dv_p[h] = dot_tn(pmix[h], grad)
            grad = rgrad[h]
            dmix = (dot_nt(grad, pairs(rv, h)) * mask_r).astype(BF16)
            across = [dot_nt(grad[r * count : (r + 1) * count], st[0, 1 + r, h].astype(BF16)) for r in range(2)]
            queries = dot_nn(dmix, pairs(rk, h)) + rstep[h] * jnp.concatenate(across, axis=0)
            dk_r[h] = dot_tn(dmix, pairs(rq, h))
            dv_r[h] = dot_tn(rmix[h], grad)
            for r in range(2):
                rdq[r, h] = queries[r * count : (r + 1) * count].astype(BF16)

    bwd.column(0)
    bwd.column(1)
    bwd.column(2)
    bases_0, totals_0 = bwd.columns(1)
    bwd.spread(1, bases_0, None)
    bases_1, totals_1 = bwd.columns(2)
    bases, _ = bwd.columns(0)
    bwd.spread(0, bases, [a + b for a, b in zip(totals_0, totals_1)])
    bwd.spread(2, bases_1, None)

    def responses(r):
        bwd.ready(1 + r)
        part = slice(r * count, (r + 1) * count)
        for h in range(heads):
            later = st[1, 1 + r, h].astype(BF16)
            fade = power(h, count - 1.0 - place_p)[:count]
            rdk[r, h] = (dk_r[h, part, :] + fade * dot_nt(rv[r, h], later)).astype(BF16)
            rdv[r, h] = (dv_r[h, part, :] + fade * dot_nn(rk[r, h], later)).astype(BF16)

    ny, nx = grid[1], grid[0]

    def sent(part, sem):
        fwd.copy(part, part, sem, sem, ahead.partner()).wait_send()

    sent(pair, c_s)
    sent(csend.at[:, :, pl.ds(0, ny - 1)], a1_s)
    sent(tx.at[:, :, pl.ds(0, nx - 1)], x_s)
    sent(stat.at[:, pl.ds(0, nz - 1)], z_s)
    bwd.finish(1)
    responses(0)
    bwd.finish(0)
    bwd.finish(2)
    bwd.ready(0)
    with jax.named_scope("end"):
        for h in range(heads):
            later = st[1, 0, h].astype(BF16)
            fade = power(h, tokens - 1.0 - place_p)
            pdk[h] = (dk_p[h] + fade * dot_nt(pv[h], later)).astype(BF16)
            pdv[h] = (dv_p[h] + fade * dot_nn(pk[h], later)).astype(BF16)
    responses(1)
    sent(psend.at[:, :, pl.ds(0, ny - 1)], a2_s)
    sent(fsend, f_s)


def hand_over(*refs):
    copies = [pltpu.make_async_copy(src, dst, refs[16].at[i]) for i, (src, dst) in enumerate(zip(refs[:8], refs[8:16]))]
    for copy in copies:
        copy.start()
    for copy in copies:
        copy.wait()


def shards(grid, nz, prompt_q, prompt_k, prompt_v, resp_q, resp_k, resp_v, decay_rate, norm_gain, prompt_cot, resp_cot):
    nx, ny, _ = grid
    tokens, heads, width = prompt_q.shape
    count = resp_q.shape[1]
    half, rows = width // 2, width // 2 // ny
    prompt = [jnp.transpose(a, (1, 0, 2)) for a in (prompt_q, prompt_k, prompt_v, prompt_cot)]
    resp = [jnp.transpose(a, (0, 2, 1, 3)) for a in (resp_q, resp_k, resp_v, resp_cot)]
    flat = pltpu.VMEM((heads, tokens, width), BF16)
    duo = pltpu.VMEM((2, heads, count, width), BF16)
    vmem, hbm = pl.BlockSpec(memory_space=pltpu.VMEM), pl.BlockSpec(memory_space=pltpu.HBM)
    block = (heads, tokens, width)
    scratch = [pltpu.SMEM((heads,), F32), pltpu.VMEM((heads, width), F32)]
    scratch += [pltpu.VMEM(block, BF16)] * 4 + [pltpu.VMEM((2, heads, count, width), BF16)] * 4
    scratch += [
        pltpu.VMEM((2, 3, heads, width, width), F32),
        pltpu.VMEM((2, 3, heads, half, width), F32),
        pltpu.VMEM((2, 3, ny, heads, rows, width), F32),
        pltpu.VMEM((2, 3, ny, heads, rows, width), F32),
        pltpu.VMEM((2, 3, nx, heads, rows, width), F32),
        pltpu.VMEM((2, 3, ny, heads, rows, width), F32),
        pltpu.VMEM((2, 3, ny, heads, rows, width), F32),
        pltpu.VMEM((2, 3, heads, half, width), F32),
        pltpu.VMEM((2, 3, heads, width, width), F32),
        pltpu.VMEM((3, nz, 8, width), F32),
        pltpu.VMEM(block, BF16),
        pltpu.VMEM(block, BF16),
        pltpu.VMEM(block, F32),
        pltpu.VMEM(block, F32),
        pltpu.VMEM(block, BF16),
        pltpu.VMEM(block, BF16),
        pltpu.VMEM(block, F32),
        pltpu.VMEM(block, F32),
        pltpu.VMEM(block, F32),
        pltpu.VMEM(block, F32),
    ]
    scratch += [pltpu.VMEM(block, BF16)] * 2 + [pltpu.VMEM(block, F32)] * 4
    dma = pltpu.SemaphoreType.DMA
    scratch += [dma((10,))] + [dma, dma((2, 3))] * 5 + [dma, dma((3,))]
    scratch += [pltpu.SemaphoreType.REGULAR((max(1, len(reaching(nz))), 2))]
    out = pl.pallas_call(
        functools.partial(kernel, grid, nz),
        out_shape=(flat, duo, flat, flat, flat, duo, duo, duo),
        in_specs=[hbm] * 10,
        out_specs=(vmem,) * 8,
        scratch_shapes=scratch,
        compiler_params=pltpu.CompilerParams(collective_id=0, has_side_effects=True, vmem_limit_bytes=40 << 20),
    )(*(pltpu.with_memory_space_constraint(a, pltpu.HBM) for a in (decay_rate, norm_gain, *prompt, *resp)))
    out = pl.pallas_call(
        hand_over,
        out_shape=tuple(jax.ShapeDtypeStruct(a.shape, a.dtype) for a in out),
        in_specs=[vmem] * 8,
        out_specs=(hbm,) * 8,
        scratch_shapes=[dma((8,))],
        compiler_params=pltpu.CompilerParams(vmem_limit_bytes=8 << 20),
    )(*out)
    return tuple(
        jnp.transpose(a, (1, 0, 2)) if a.ndim == 3 else jnp.transpose(a, (0, 2, 1, 3)) for a in out
    )


def solution(mesh):
    flat, duo = P("ctx", "head", None), P(None, "ctx", "head", None)
    return jax.shard_map(
        functools.partial(shards, GRID, mesh.shape["head"]),
        mesh=mesh,
        in_specs=(flat, flat, flat, duo, duo, duo, P("head"), P("head", None), flat, duo),
        out_specs=(flat, duo, flat, flat, flat, duo, duo, duo),
        check_vma=False,
    )
```
